32 devices in a mesh: head: 8 (over z, y), qblk: 4 (over x, core).
Axes of the slice: x: 2, y: 2, z: 4, core: 2. Of those that a mesh axis runs over, the one named last changes fastest.
Arguments:
- residual: bfloat16 [1024, 2048], P(('qblk', 'head')), may hold values from -6 to 6
- queries: bfloat16 [1024, 4096], P('qblk', 'head'), may hold values from -30 to 30
- key_cache: bfloat16 [4, 2048, 128], P(None, 'qblk'), may hold values from -6 to 6
- value_cache: bfloat16 [4, 2048, 128], P(None, 'qblk'), may hold values from -6 to 6
- visible_len: int32 [1024], P('qblk'), may hold values from 256 to 2048
- out_weight: bfloat16 [4096, 2048], P('head'), may hold values from -0.5 to 0.5
- norm_gain: float32 [2048], replicated, may hold values from 0.1 to 1.9
- expert_ids: int32 [1024, 8], P(('qblk', 'head')), may hold values from 0 to 31, all different within a row; in each aligned block of 32 rows (0 to 31, 32 to 63, ...) at most 16 rows name the same one
- route_weights: float32 [1024, 8], P(('qblk', 'head')), may hold values from 0.02 to 0.3
- w_gate: bfloat16 [32, 2048, 768], P(('head', 'qblk')), may hold values from -0.125 to 0.125
- w_up: bfloat16 [32, 2048, 768], P(('head', 'qblk')), may hold values from -0.125 to 0.125
- w_down: bfloat16 [32, 768, 2048], P(('head', 'qblk')), may hold values from -0.21875 to 0.21875
Outputs:
- layer_out: bfloat16 [1024, 2048], P(('qblk', 'head'))
The draws below stay inside these ranges and needn't reach their ends.
Inputs may be any that keep to these rules, and one draw needn't show every extreme that they name: `expert_ids`: each row names 8 different experts; in each aligned block of 32 rows (the rows of one device) no expert is named more than 16 times, and some block names some expert exactly 16 times.
All inputs are finite; a program needn't handle non-finite values.
Results may differ from the reference program's by a relative error of at most 0.012.
Values may be sent and summed in bfloat16 or wider, within the bound.
No kernel may reach another device: no remote copies, remote signals or barrier semaphores. Data moves between devices by JAX's collectives and lax.ppermute only.
A program may use at most 64 MiB of HBM per device.

```python
import math
import jax
import jax.numpy as jnp
import numpy as np
from jax import lax

D = 2048
QH = 32
KVH = 4
HD = 128
FF = 768
TOPK = 8
EXPERTS = 32
KEYS = 2048
TOK_DEV = 32
TOKENS = 1024
CAP = 16


def base_keys(key):
    raw = jnp.clip(jax.random.normal(jax.random.fold_in(key, 11), (KVH, KEYS, HD), jnp.float32), -6.0, 6.0)
    return raw.astype(jnp.bfloat16)


def draw_key_cache(key, part):
    return base_keys(key)


def draw_queries(key, part):
    drawn = jnp.clip(jax.random.normal(jax.random.fold_in(key, 23), (TOKENS, QH, HD), jnp.float32), -6.0, 6.0)
    return drawn.reshape(TOKENS, QH * HD).astype(jnp.bfloat16)


def set_ends(values, stream_key, least, largest):
    longest = values.shape.index(max(values.shape))
    spots = []
    for shift in (0, 1):
        where = [jax.random.randint(jax.random.fold_in(stream_key, axis), (), 0, length) for axis, length in enumerate(values.shape)]
        where[longest] = (where[longest] + shift) % values.shape[longest]
        spots.append(tuple(where))
    return values.at[spots[0]].set(least).at[spots[1]].set(largest)


def block_scale(stream_key, shape, pieces, smallest, top_value):
    def one(dim, parts):
        draws = jax.random.uniform(jax.random.fold_in(jax.random.fold_in(stream_key, 6), dim), (parts,), jnp.float32, smallest / len(pieces), top_value / len(pieces))
        return jnp.repeat(jnp.exp(draws), shape[dim] // parts).reshape((-1,) + (1,) * (len(shape) - dim - 1))

    factor_of = one(*pieces[0])
    for cut in pieces[1:]:
        factor_of = factor_of * one(*cut)
    return factor_of


def routed_block(key, own, number, rows, count, top, most, slope):
    sequence = jax.random.permutation(key, count)
    heavy_load, ordinary = load_shares(count, rows * top, most, slope, True), load_shares(count, rows * top, most, slope, False)
    places = jnp.arange(count)

    def named(sizes, rotation):
        used = int((sizes > 0).sum())
        fixed = max(1, used // 4)
        moved = fixed + (places - fixed + rotation * (used - fixed)) % max(1, count - fixed)
        return jnp.zeros((count,), jnp.int32).at[sequence[jnp.where(places < fixed, places, moved)]].set(jnp.asarray(sizes, jnp.int32))

    sizes = jnp.where(number % 4 == 0, named(heavy_load, number // 4), named(ordinary, number - number // 4 - 1))
    mixed = jax.random.permutation(jax.random.fold_in(own, 3), count)
    giver, receiver = mixed[0:count // 2 * 2:2], mixed[1:count // 2 * 2:2]
    room = jnp.minimum(sizes[giver] - 1, most - sizes[receiver]) // 2
    room = jnp.where((giver == sequence[0]) | (receiver == sequence[0]) | (sizes[receiver] == 0), 0, jnp.maximum(room, 0))
    moved = jax.random.randint(jax.random.fold_in(own, 4), (count // 2,), 0, 1 << 20) % (room + 1)
    sizes = sizes.at[giver].add(-moved).at[receiver].add(moved)
    items = jnp.searchsorted(jnp.cumsum(sizes), jnp.arange(rows * top), side="right").astype(jnp.int32)
    table = items.reshape(top, rows).T
    table = table[jax.random.permutation(jax.random.fold_in(own, 1), rows)]
    rotation = jax.random.randint(jax.random.fold_in(own, 2), (rows, 1), 0, top)
    return jnp.take_along_axis(table, (jnp.arange(top)[None, :] + rotation) % top, axis=1)


def load_shares(number_of, total, reach, skew, full):
    portions = [(1 << 20) // math.isqrt(standing ** skew) + 1 for standing in range(1, number_of + 1)]
    largest = reach if full else min(reach, max(-(-total // number_of), total * portions[0] // sum(portions)))
    least = 1 if total - largest >= number_of - 1 else 0
    holding, rest = [largest] + [least] * (number_of - 1), total - largest - least * (number_of - 1)
    while rest > 0:
        candidates = [i for i in range(1, number_of) if holding[i] < largest] or [i for i in range(1, number_of) if holding[i] < reach]
        pool, left = sum([portions[i] for i in candidates]), rest
        for i in candidates:
            more = min(reach - holding[i], max(1, left * portions[i] // pool), rest)
            holding[i] = holding[i] + more
            rest = rest - more
    return np.array(holding)


def centred(key, shape, width, bound, cuts=(), kind=jnp.bfloat16):
    result = jax.random.normal(key, shape, jnp.float32) * width
    if len(cuts) > 0:
        result = block_scale(key, shape, cuts, -0.22, 0.18) * result
    return jnp.clip(result, min=-bound, max=bound).astype(kind)


def setup_inputs(seed: int = 0) -> dict:
    key_list = jax.random.split(jax.random.key(seed), 13)
    residual = centred(key_list[0], (TOKENS, D), 1.0, 6.0, ((0, 32),))
    queries = draw_queries(jax.random.fold_in(key_list[12], 71), 0)
    key_cache = draw_key_cache(jax.random.fold_in(key_list[12], 71), 0)
    value_cache = centred(key_list[3], (KVH, KEYS, HD), 1.0, 6.0, ((1, 4),))
    visible_len = set_ends(jax.random.randint(key_list[4], (TOKENS,), KEYS // 8, KEYS + 1), jax.random.fold_in(key_list[4], 1), KEYS // 8, KEYS).astype(jnp.int32)
    out_weight = centred(key_list[5], (QH * HD, D), HD ** -0.5, 0.5, ((0, 8),))
    norm_gain = jnp.clip(1.0 + 0.18 * jax.random.normal(key_list[6], (D,), jnp.float32), 0.1, 1.9)
    expert_ids_keys = jax.random.split(jax.random.fold_in(key_list[7], 1), TOKENS // TOK_DEV)
    expert_ids_turns = jax.random.permutation(jax.random.fold_in(key_list[7], 3), TOKENS // TOK_DEV)
    expert_ids = jax.vmap(lambda own, number: routed_block(jax.random.fold_in(key_list[7], 2), own, number, TOK_DEV, EXPERTS, TOPK, CAP, 2))(expert_ids_keys, expert_ids_turns).reshape((TOKENS, TOPK))
    route_weights = jnp.clip(0.02 + 0.28 * jax.random.uniform(key_list[8], (TOKENS, TOPK), jnp.float32) ** block_scale(key_list[8], (TOKENS, TOPK), ((0, 32),), -0.2, 0.2), 0.02, 0.3)
    w_gate = centred(key_list[9], (EXPERTS, D, FF), D ** -0.5, 0.125, ((0, 32),))
    w_up = centred(key_list[10], (EXPERTS, D, FF), D ** -0.5, 0.125, ((0, 32),))
    w_down = centred(key_list[11], (EXPERTS, FF, D), FF ** -0.5, 0.21875, ((0, 32),))
    return dict(residual=residual, queries=queries, key_cache=key_cache, value_cache=value_cache, visible_len=visible_len, out_weight=out_weight, norm_gain=norm_gain, expert_ids=expert_ids, route_weights=route_weights, w_gate=w_gate, w_up=w_up, w_down=w_down)


def reference(residual, queries, key_cache, value_cache, visible_len, out_weight, norm_gain, expert_ids, route_weights, w_gate, w_up, w_down):
    group_size = QH // KVH
    score_scale = HD ** (-0.5)
    key_pos = jnp.arange(KEYS, dtype=jnp.int32)
    visible = key_pos[None, :] < visible_len[:, None]

    def one_head(head_idx):
        head_query = lax.dynamic_slice_in_dim(queries, head_idx * HD, HD, 1)
        kv_idx = head_idx // group_size
        head_keys = key_cache[kv_idx]
        head_values = value_cache[kv_idx]
        scores = jnp.dot(head_query, head_keys.T, preferred_element_type=jnp.float32) * score_scale
        scores = jnp.where(visible, scores, -jnp.inf)
        row_max = lax.optimization_barrier(jnp.max(scores, axis=1, keepdims=True))
        exp_scores = jnp.where(visible, jnp.exp(scores - row_max), 0.0)
        row_sum = lax.optimization_barrier(jnp.sum(exp_scores, axis=1, keepdims=True))
        head_out = jnp.dot(exp_scores.astype(jnp.bfloat16), head_values, preferred_element_type=jnp.float32) / row_sum
        return head_out.astype(jnp.bfloat16)
    stacked = lax.map(one_head, jnp.arange(QH, dtype=jnp.int32))
    attended = jnp.transpose(stacked, (1, 0, 2)).reshape(TOKENS, QH * HD)
    hidden_state = residual.astype(jnp.float32) + jnp.dot(attended, out_weight, preferred_element_type=jnp.float32)
    mean_square = lax.optimization_barrier(jnp.mean(hidden_state * hidden_state, axis=1, keepdims=True))
    normed = (hidden_state * lax.rsqrt(mean_square + 1e-06) * norm_gain).astype(jnp.bfloat16)
    blocks = TOKENS // TOK_DEV
    entries = TOK_DEV * TOPK
    flat_ids = expert_ids.reshape(blocks, entries)
    expert_range = jnp.arange(EXPERTS, dtype=jnp.int32)
    onehot = (flat_ids[:, :, None] == expert_range[None, None, :]).astype(jnp.int32)
    running_rank = (jnp.cumsum(onehot, axis=1) - 1).astype(jnp.int32)
    slot_pos = lax.optimization_barrier(jnp.sum(onehot * running_rank, axis=2)).astype(jnp.int32)
    block_idx = jnp.arange(blocks, dtype=jnp.int32)[:, None]
    entry_idx = jnp.arange(entries, dtype=jnp.int32)[None, :]
    token_idx = (block_idx * TOK_DEV + entry_idx // TOPK).astype(jnp.int32)
    column = (block_idx * CAP + slot_pos).astype(jnp.int32)
    table = jnp.full((EXPERTS, blocks * CAP), TOKENS, jnp.int32).at[flat_ids, column].set(token_idx)
    weight_table = jnp.zeros((EXPERTS, blocks * CAP), jnp.float32).at[flat_ids, column].set(route_weights.reshape(blocks, entries))
    padded = jnp.concatenate([normed, jnp.zeros((1, D), jnp.bfloat16)], axis=0)

    def serve(total, items):
        rows_idx, row_weight, gate_matrix, up_matrix, down_matrix = items
        chosen = padded[rows_idx]
        gate_act = jnp.dot(chosen, gate_matrix, preferred_element_type=jnp.float32)
        up_act = jnp.dot(chosen, up_matrix, preferred_element_type=jnp.float32)
        hidden = (jax.nn.silu(gate_act) * up_act).astype(jnp.bfloat16)
        expert_out = jnp.dot(hidden, down_matrix, preferred_element_type=jnp.float32).astype(jnp.bfloat16)
        total = total.at[rows_idx].add(row_weight[:, None] * expert_out.astype(jnp.float32))
        return (total, None)
    start_total = jnp.zeros((TOKENS + 1, D), jnp.float32)
    mixed, unused = lax.scan(serve, start_total, (table, weight_table, w_gate, w_up, w_down))
    return (hidden_state + mixed[:TOKENS]).astype(jnp.bfloat16)
```

```python
import jax
import jax.numpy as jnp
from jax import lax
from jax.sharding import PartitionSpec as P

QH = 32
KVH = 4
HD = 128
F32 = jnp.float32
BF16 = jnp.bfloat16
LANES = 128


def swap(v, link):
    axis, mask = link
    return lax.ppermute(v, axis, [(i, i ^ mask) for i in range(lax.axis_size(axis))])


def links():
    core, x, y, z = ("qblk", 1), ("qblk", 2), ("head", 1), ("head", 2)
    far = []
    for axis in ("head", "qblk"):
        bit = 4
        while bit < lax.axis_size(axis):
            far.append((axis, bit | bit >> 1))
            bit *= 2
    return core, x, y, z, far


def head_order(me):
    _, _, y, z, far = links()
    order = [0]
    for axis, mask in [link for link in far if link[0] == "head"] + [y, z]:
        order = order + [o ^ mask for o in order]
    return [me ^ o for o in order]


def column_cuts(width):
    tiles = width // LANES
    first = -(-tiles // 3)
    first += first % 2
    return (0, first * LANES, 2 * first * LANES, width)


def spread(block, dims, far):
    for link in far:
        block = jnp.concatenate([block, swap(block, link)], axis=0)
    cuts = column_cuts(block.shape[1] - LANES)
    cuts = (*cuts[:3], block.shape[1])
    parts = [block[None, None, None, :, cuts[i] : cuts[i + 1]] for i in range(3)]
    for stage in range(3):
        got = [swap(parts[i], dims[(i + stage) % 3]) for i in range(3)]
        parts = [jnp.concatenate([parts[i], got[i]], axis=(i + stage) % 3) for i in range(3)]
    return [p.reshape(-1, p.shape[-1]) for p in parts]


def halves(v, axis):
    return lax.index_in_dim(v, 0, axis), lax.index_in_dim(v, 1, axis)


def fold(parts, dims, far, rows):
    parts = [p.reshape(2, 2, 2, -1, p.shape[-1]) for p in parts]
    for stage in range(3):
        axes = [(i + stage) % 3 for i in range(3)]
        split = [halves(parts[i], axes[i]) for i in range(3)]
        got = [swap(split[i][1].astype(BF16), dims[axes[i]]) for i in range(3)]
        parts = [split[i][0] + got[i].astype(F32) for i in range(3)]
    total = jnp.concatenate([p.reshape(-1, p.shape[-1]) for p in parts], axis=1)
    return fold_far(total, far)


def fold_far(total, far):
    for link in reversed(far):
        half = total.shape[0] // 2
        total = total[:half] + swap(total[half:].astype(BF16), link).astype(F32)
    return total


def attend(keys, values, query_heads, visible_len):
    scores = jnp.einsum(
        "thd,nd->thn", query_heads, keys, preferred_element_type=F32
    ) * HD ** (-0.5)
    key_pos = jnp.arange(keys.shape[0], dtype=jnp.int32)
    visible = key_pos[None, None, :] < visible_len[:, None, None]
    scores = jnp.where(visible, scores, -1e30)
    top = jnp.max(scores, axis=2)
    weights = jnp.where(visible, jnp.exp(scores - top[:, :, None]), 0.0)
    denom = jnp.sum(weights, axis=2)
    mixed = jnp.einsum("thn,nd->thd", weights.astype(BF16), values, preferred_element_type=F32)
    return (mixed / denom[:, :, None]).astype(BF16)


def gather_keys(key_cache, value_cache, kv_index):
    own = jnp.concatenate(
        [
            lax.dynamic_index_in_dim(key_cache, kv_index, 0, keepdims=False),
            lax.dynamic_index_in_dim(value_cache, kv_index, 0, keepdims=False),
        ],
        axis=1,
    )[None]
    count = lax.axis_size("qblk")
    me = lax.axis_index("qblk")
    core, x, _, _, far = links()
    order = [0]
    for link in [link for link in far if link[0] == "qblk"] + [x, core]:
        own = jnp.concatenate([own, swap(own, link)], axis=0)
        order = order + [o ^ link[1] for o in order]
    where = [order.index(i) for i in range(count)]
    slot = jnp.array(where, jnp.int32)
    blocks = [lax.dynamic_index_in_dim(own, slot[me ^ i], 0, keepdims=False) for i in range(count)]
    both = jnp.concatenate(blocks, axis=0)
    return both[:, :HD], both[:, HD:]


def expert(parts, route, gate_matrix, up_matrix, down_matrix, mine):
    top = 8
    ids = route[:, :top]
    weight = sum(route[:, top * i : top * (i + 1)].astype(F32) for i in range(1, 4))
    scale = jnp.sum(jnp.where(ids == mine.astype(BF16), weight, 0.0), axis=1, keepdims=True)
    rows = jnp.concatenate(parts, axis=1)
    gate_act = jnp.dot(rows, gate_matrix, preferred_element_type=F32)
    up_act = jnp.dot(rows, up_matrix, preferred_element_type=F32)
    hidden = (jax.nn.silu(gate_act) * up_act).astype(BF16)
    return jnp.dot(hidden, down_matrix, preferred_element_type=F32) * scale


def route_columns(expert_ids, route_weights):
    rest, columns = route_weights, [expert_ids.astype(BF16)]
    for _ in range(3):
        piece = lax.reduce_precision(rest, 8, 7)
        columns.append(piece.astype(BF16))
        rest = rest - piece
    table = jnp.concatenate(columns, axis=1)
    return jnp.pad(table, ((0, 0), (0, LANES - table.shape[1])))


def per_device(
    residual,
    queries,
    key_cache,
    value_cache,
    visible_len,
    out_weight,
    norm_gain,
    expert_ids,
    route_weights,
    w_gate,
    w_up,
    w_down,
):
    core, x, y, z, far = links()
    head_me = lax.axis_index("head")
    head_count = lax.axis_size("head")
    token_rows, width = residual.shape
    local_heads = queries.shape[1] // HD
    kv_index = head_me * local_heads // (QH // KVH)
    keys, values = gather_keys(key_cache, value_cache, kv_index)

    order = head_order(head_me)
    query_blocks = queries.reshape(head_count, token_rows, -1)
    len_blocks = visible_len.reshape(head_count, token_rows)
    query_rel = jnp.concatenate([lax.dynamic_index_in_dim(query_blocks, o, 0, False) for o in order])
    len_rel = jnp.concatenate([lax.dynamic_index_in_dim(len_blocks, o, 0, False) for o in order])
    attended = attend(keys, values, query_rel.reshape(-1, local_heads, HD), len_rel)
    attended = attended.reshape(head_count * token_rows, -1)
    half = width // 2
    parts = []
    for i in range(2):
        part = jnp.dot(
            attended, out_weight[:, i * half : (i + 1) * half], preferred_element_type=F32
        ).reshape(2, 2, -1, half)
        parts.append(part)
    pair = (z, y)
    for stage in range(2):
        split = [halves(parts[i], (i + stage) % 2) for i in range(2)]
        got = [swap(split[i][1].astype(BF16), pair[(i + stage) % 2]) for i in range(2)]
        parts = [split[i][0] + got[i].astype(F32) for i in range(2)]
    total = jnp.concatenate([p.reshape(-1, half) for p in parts], axis=1)
    projected = fold_far(total, [link for link in far if link[0] == "head"])

    hidden_state = residual.astype(F32) + projected
    mean_square = jnp.mean(hidden_state * hidden_state, axis=1, keepdims=True)
    normed = (hidden_state * lax.rsqrt(mean_square + 1e-06) * norm_gain).astype(BF16)

    block = jnp.concatenate([normed, route_columns(expert_ids, route_weights)], axis=1)
    dims = (x, y, z)
    near = spread(block, dims, far)
    other = [swap(p, core) for p in near]
    mine = head_me * lax.axis_size("qblk") + lax.axis_index("qblk")

    def run(pieces):
        last = pieces[2].shape[1] - LANES
        rows = [pieces[0], pieces[1], pieces[2][:, :last]]
        return expert(rows, pieces[2][:, last:], w_gate[0], w_up[0], w_down[0], mine)

    sent = swap(run(other).astype(BF16), core)
    total = run(near) + sent.astype(F32)
    cuts = column_cuts(width)
    parts = [total[:, cuts[i] : cuts[i + 1]] for i in range(3)]
    mix = fold(parts, dims, far, token_rows)
    return (hidden_state + mix).astype(BF16)


def solution(mesh):
    in_specs = (
        P(("qblk", "head"), None),
        P("qblk", "head"),
        P(None, "qblk", None),
        P(None, "qblk", None),
        P("qblk"),
        P("head", None),
        P(),
        P(("qblk", "head"), None),
        P(("qblk", "head"), None),
        P(("head", "qblk"), None, None),
        P(("head", "qblk"), None, None),
        P(("head", "qblk"), None, None),
    )
    out_specs = P(("qblk", "head"), None)
    return jax.shard_map(
        per_device, mesh=mesh, in_specs=in_specs, out_specs=out_specs, check_vma=False
    )
```

```python
import functools
import math

import jax
import jax.numpy as jnp
from jax import lax
from jax.experimental import pallas as pl
from jax.experimental.pallas import tpu as pltpu
from jax.sharding import PartitionSpec as P

QH = 32
KVH = 4
HD = 128
F32 = jnp.float32
BF16 = jnp.bfloat16
LANES = 128
TILE = 256
MIB = 1 << 20


def swap(v, link):
    axis, mask = link
    return lax.ppermute(v, axis, [(i, i ^ mask) for i in range(lax.axis_size(axis))])


def links():
    core, x, y, z = ("qblk", 1), ("qblk", 2), ("head", 1), ("head", 2)
    far = []
    for axis in ("head", "qblk"):
        bit = 4
        while bit < lax.axis_size(axis):
            far.append((axis, bit | bit >> 1))
            bit *= 2
    return core, x, y, z, far


def masks_of(chosen):
    order = [0]
    for _, mask in chosen:
        order = order + [o ^ mask for o in order]
    return order


def column_cuts(width):
    tiles = width // LANES
    first = -(-tiles // 3)
    first += first % 2
    return (0, first * LANES, 2 * first * LANES, width)


def call(kernel, outs, args, specs, scratch, flops, grant):
    nbytes = sum(math.prod(a.shape) * a.dtype.itemsize for a in (*args, *outs))
    return pl.pallas_call(
        kernel,
        out_shape=outs,
        in_specs=specs,
        out_specs=[pl.BlockSpec(memory_space=pltpu.VMEM)] * len(outs),
        scratch_shapes=scratch,
        compiler_params=pltpu.CompilerParams(vmem_limit_bytes=grant),
        cost_estimate=pl.CostEstimate(flops=flops, bytes_accessed=nbytes, transcendentals=0),
    )(*args)


IN_VMEM = pl.BlockSpec(memory_space=pltpu.VMEM)
IN_SMEM = pl.BlockSpec(memory_space=pltpu.SMEM)


def attention_kernel(cfg, where, query, lens, *refs):
    kv, out_weight = refs[: cfg["blocks"]], refs[cfg["blocks"]]
    send_a, keep_a, send_b, keep_b, stacked, scores, attended = refs[cfg["blocks"] + 1 :]
    token_rows, heads, near = cfg["token_rows"], cfg["heads"], cfg["near"]
    head_me, qblk_me = where[0], where[1]
    tile = 2 * near
    keys = kv[0].shape[0]
    factor = HD ** (-0.5) * math.log2(math.e)
    group = max(1, TILE // tile)
    half = out_weight.shape[1] // 2
    for z in (1, 0):
        starts = []
        for o in cfg["order"][z]:
            starts.append(pl.multiple_of((head_me ^ o) * token_rows, token_rows))
        span = jnp.concatenate([lens[pl.ds(s, token_rows), :] for s in starts], axis=0)
        span = jnp.concatenate([span] * group, axis=0)
        for first in range(0, heads, group):
            for h in range(group):
                lanes = pl.ds((first + h) * HD, HD)
                for i, s in enumerate(starts):
                    rows = pl.ds(h * tile + i * token_rows, token_rows)
                    stacked[rows, :] = query[pl.ds(s, token_rows), lanes]
            q = stacked[...]
            top = None
            for b in range(cfg["blocks"]):
                s = lax.dot_general(
                    q, kv[b][:, :HD], (((1,), (1,)), ((), ())), preferred_element_type=F32
                )
                base = (qblk_me ^ cfg["offsets"][b]) * keys
                pos = base + lax.broadcasted_iota(jnp.int32, s.shape, 1)
                s = jnp.where(pos < span, s, -1e30)
                scores[:, b * keys : (b + 1) * keys] = s
                here = jnp.max(s, axis=1, keepdims=True)
                top = here if top is None else jnp.maximum(top, here)
            denom, mixed = 0.0, 0.0
            for b in range(cfg["blocks"]):
                s = scores[:, b * keys : (b + 1) * keys]
                w = jnp.exp2((s - top) * factor)
                denom = denom + jnp.sum(w, axis=1, keepdims=True)
                mixed = mixed + jnp.dot(
                    w.astype(BF16), kv[b][:, HD:], preferred_element_type=F32
                )
            result = (mixed / denom).astype(BF16)
            for h in range(group):
                attended[:, (first + h) * HD : (first + h + 1) * HD] = result[
                    h * tile : (h + 1) * tile
                ]
        a = attended[...]
        for col in range(0, 2 * half, TILE):
            p = jnp.dot(a, out_weight[:, col : col + TILE], preferred_element_type=F32)
            for y in (0, 1):
                rows = p[y * near : (y + 1) * near]
                if col < half:
                    at = slice(col, col + TILE)
                    if z:
                        send_a[y, :, at] = rows.astype(BF16)
                    else:
                        keep_a[y, :, at] = rows
                else:
                    at = slice(col - half, col - half + TILE)
                    if y:
                        send_b[z, :, at] = rows.astype(BF16)
                    else:
                        keep_b[z, :, at] = rows


def attention(queries, visible_len, kv, offsets, out_weight, token_rows):
    _, _, y, z, far = links()
    tokens, lanes = queries.shape
    heads = lanes // HD
    far = [link for link in far if link[0] == "head"]
    order = masks_of([*far, y, z])
    blocks = len(order) // 2
    near = blocks // 2 * token_rows
    half = out_weight.shape[1] // 2
    cfg = dict(
        blocks=len(kv),
        token_rows=token_rows,
        heads=heads,
        near=near,
        order=(order[:blocks], order[blocks:]),
        offsets=offsets,
    )
    tile = 2 * near
    rows = max(1, TILE // tile) * tile
    where = jnp.stack([lax.axis_index("head"), lax.axis_index("qblk")])
    keys = kv[0].shape[0] * len(kv)
    outs = [
        jax.ShapeDtypeStruct((2, near, half), kind) for kind in (BF16, F32, BF16, F32)
    ]
    return call(
        functools.partial(attention_kernel, cfg),
        outs,
        [where, queries, visible_len.reshape(tokens, 1), *kv, out_weight],
        [IN_SMEM] + [IN_VMEM] * (3 + len(kv)),
        [
            pltpu.VMEM((rows, HD), BF16),
            pltpu.VMEM((rows, keys), F32),
            pltpu.VMEM((tile, lanes), BF16),
        ],
        4 * tokens * heads * keys * HD + 2 * tokens * lanes * 2 * half,
        32 * MIB,
    )


def gather_keys(key_cache, value_cache, kv_index):
    own = jnp.concatenate(
        [
            lax.dynamic_index_in_dim(key_cache, kv_index, 0, keepdims=False),
            lax.dynamic_index_in_dim(value_cache, kv_index, 0, keepdims=False),
        ],
        axis=1,
    )
    core, x, _, _, far = links()
    chosen = [link for link in far if link[0] == "qblk"] + [x, core]
    blocks = [own]
    for link in chosen:
        blocks = blocks + [swap(b, link) for b in blocks]
    return blocks, masks_of(chosen)


def reduce_heads(send_a, keep_a, send_b, keep_b):
    _, _, y, z, far = links()
    got_a, got_b = swap(send_a, z), swap(send_b, y)

    def second(keep, got, link):
        sent = swap((keep[1] + got[1].astype(F32)).astype(BF16), link)
        return keep[0] + got[0].astype(F32) + sent.astype(F32)

    total = jnp.concatenate([second(keep_a, got_a, y), second(keep_b, got_b, z)], axis=1)
    return fold_far(total, [link for link in far if link[0] == "head"])


def fold_far(total, far):
    for link in reversed(far):
        half = total.shape[0] // 2
        total = total[:half] + swap(total[half:].astype(BF16), link).astype(F32)
    return total


def spread(block, dims, far):
    for link in far:
        block = jnp.concatenate([block, swap(block, link)], axis=0)
    cuts = column_cuts(block.shape[1] - LANES)
    cuts = (*cuts[:3], block.shape[1])
    parts = [block[None, None, None, :, cuts[i] : cuts[i + 1]] for i in range(3)]
    for stage in range(2):
        got = [swap(parts[i], dims[(i + stage) % 3]) for i in range(3)]
        parts = [jnp.concatenate([parts[i], got[i]], axis=(i + stage) % 3) for i in range(3)]
    got = [swap(parts[i], dims[(i + 2) % 3]) for i in range(3)]
    return parts, got


def expert_kernel(cfg, mine, *refs):
    own, got, (gate, up, down) = refs[:3], refs[3:6], refs[6:9]
    refs = refs[9:]
    cuts, last = cfg["cuts"], cfg["final"]
    if last:
        other, refs = refs[0], refs[1:]
        sends, keeps, hidden = refs[:3], refs[3:6], refs[6]
    else:
        out, hidden = refs
    rows = own[0].shape[3]
    top = cfg["top"]
    places = [(x, y, z) for x in (0, 1) for y in (0, 1) for z in (0, 1)]
    batch = max(1, TILE // rows)

    def block(i, place):
        axis = (i + 2) % 3
        src = got[i] if place[axis] else own[i]
        return src[tuple(0 if a == axis else place[a] for a in range(3))]

    for start in range(0, 8, batch):
        group = places[start : start + batch]
        lhs = [jnp.concatenate([block(i, p) for p in group], axis=0) for i in range(3)]
        width = lhs[2].shape[1] - LANES
        route = lhs[2][:, width:].astype(F32)
        lhs[2] = lhs[2][:, :width]
        lane = lax.broadcasted_iota(jnp.int32, route.shape, 1)
        hit = (route == mine[0].astype(F32)) & (lane < top)
        weight = sum(pltpu.roll(route, LANES - top * k, 1) for k in (1, 2, 3))
        scale = jnp.sum(jnp.where(hit, weight, 0.0), axis=1, keepdims=True)
        for f in range(0, hidden.shape[1], TILE):

            def act(matrix):
                return sum(
                    jnp.dot(
                        lhs[i], matrix[0, cuts[i] : cuts[i + 1], f : f + TILE],
                        preferred_element_type=F32,
                    )
                    for i in range(3)
                )

            g = act(gate)
            u = act(up)
            hidden[:, f : f + TILE] = (g / (1.0 + jnp.exp(-g)) * u).astype(BF16)
        h = hidden[...]
        for i in range(3):
            for col in range(cuts[i], cuts[i + 1], TILE):
                y = jnp.dot(h, down[0, :, col : col + TILE], preferred_element_type=F32) * scale
                if not last:
                    at = start * rows
                    out[at : at + y.shape[0], col : col + TILE] = y.astype(BF16)
                    continue
                for n, place in enumerate(group):
                    at = (start + n) * rows
                    v = y[n * rows : (n + 1) * rows] + other[
                        at : at + rows, col : col + TILE
                    ].astype(F32)
                    rest = tuple(place[a] for a in range(3) if a != i)
                    lanes = slice(col - cuts[i], col - cuts[i] + TILE)
                    if place[i]:
                        sends[i][(*rest, slice(None), lanes)] = v.astype(BF16)
                    else:
                        keeps[i][(*rest, slice(None), lanes)] = v


def expert(own, got, matrices, mine, top, other=None):
    rows = own[0].shape[3]
    width = sum(p.shape[4] for p in own) - LANES
    cuts = column_cuts(width)
    hidden = matrices[0].shape[2]
    cfg = dict(cuts=cuts, final=other is not None, top=top)
    if other is None:
        outs = [jax.ShapeDtypeStruct((8 * rows, width), BF16)]
    else:
        outs = [
            jax.ShapeDtypeStruct((2, 2, rows, cuts[i + 1] - cuts[i]), kind)
            for kind in (BF16, F32)
            for i in range(3)
        ]
    args = [mine, *own, *got, *matrices] + ([] if other is None else [other])
    return call(
        functools.partial(expert_kernel, cfg),
        outs,
        args,
        [IN_SMEM] + [IN_VMEM] * (len(args) - 1),
        [pltpu.VMEM((max(1, TILE // rows) * rows, hidden), BF16)],
        6 * 8 * rows * width * hidden,
        32 * MIB,
    )


def fold(sends, keeps, dims, far):
    got = [swap(sends[i], dims[i]) for i in range(3)]
    for stage in (1, 2):
        nxt = []
        for i in range(3):
            axis = (i + stage) % 3
            left = [a for a in range(3) if a not in [(i + s) % 3 for s in range(stage)]]
            at = left.index(axis)
            keep = [lax.index_in_dim(keeps[i], k, at, False) for k in (0, 1)]
            new = [lax.index_in_dim(got[i], k, at, False).astype(F32) for k in (0, 1)]
            nxt.append((keep[0] + new[0], swap((keep[1] + new[1]).astype(BF16), dims[axis])))
        keeps, got = [n[0] for n in nxt], [n[1] for n in nxt]
    total = jnp.concatenate([keeps[i] + got[i].astype(F32) for i in range(3)], axis=1)
    return fold_far(total, far)


def route_columns(expert_ids, route_weights):
    rest, columns = route_weights, [expert_ids.astype(BF16)]
    for _ in range(3):
        piece = lax.reduce_precision(rest, 8, 7)
        columns.append(piece.astype(BF16))
        rest = rest - piece
    table = jnp.concatenate(columns, axis=1)
    return jnp.pad(table, ((0, 0), (0, LANES - table.shape[1])))


def per_device(
    residual,
    queries,
    key_cache,
    value_cache,
    visible_len,
    out_weight,
    norm_gain,
    expert_ids,
    route_weights,
    w_gate,
    w_up,
    w_down,
):
    core, x, y, z, far = links()
    head_me = lax.axis_index("head")
    local_heads = queries.shape[1] // HD
    kv, offsets = gather_keys(key_cache, value_cache, head_me * local_heads // (QH // KVH))
    projected = reduce_heads(
        *attention(queries, visible_len, kv, offsets, out_weight, residual.shape[0])
    )
    hidden_state = residual.astype(F32) + projected
    mean_square = jnp.mean(hidden_state * hidden_state, axis=1, keepdims=True)
    normed = (hidden_state * lax.rsqrt(mean_square + 1e-06) * norm_gain).astype(BF16)

    block = jnp.concatenate([normed, route_columns(expert_ids, route_weights)], axis=1)
    dims = (x, y, z)
    own, got = spread(block, dims, far)
    own_c, got_c = [swap(p, core) for p in own], [swap(p, core) for p in got]
    mine = (head_me * lax.axis_size("qblk") + lax.axis_index("qblk")).reshape(1)
    matrices = (w_gate, w_up, w_down)
    top = expert_ids.shape[1]
    (for_other,) = expert(own_c, got_c, matrices, mine, top)
    outs = expert(own, got, matrices, mine, top, swap(for_other, core))
    mix = fold(outs[:3], outs[3:], dims, far)
    return (hidden_state + mix).astype(BF16)


def solution(mesh):
    in_specs = (
        P(("qblk", "head"), None),
        P("qblk", "head"),
        P(None, "qblk", None),
        P(None, "qblk", None),
        P("qblk"),
        P("head", None),
        P(),
        P(("qblk", "head"), None),
        P(("qblk", "head"), None),
        P(("head", "qblk"), None, None),
        P(("head", "qblk"), None, None),
        P(("head", "qblk"), None, None),
    )
    out_specs = P(("qblk", "head"), None)
    return jax.shard_map(
        per_device, mesh=mesh, in_specs=in_specs, out_specs=out_specs, check_vma=False
    )
```

```python
import functools
import math

import jax
import jax.numpy as jnp
from jax import lax
from jax.experimental import pallas as pl
from jax.experimental.pallas import tpu as pltpu
from jax.sharding import PartitionSpec as P


QH = 32
KVH = 4
HD = 128
F32 = jnp.float32
BF16 = jnp.bfloat16
LANES = 128
TILE = 256
MIB = 1 << 20
COVER = 2 * 10**10


def swap(v, link):
    axis, mask = link
    return lax.ppermute(v, axis, [(i, i ^ mask) for i in range(lax.axis_size(axis))])


def links():
    core, x, y, z = ("qblk", 1), ("qblk", 2), ("head", 1), ("head", 2)
    far = []
    for axis in ("head", "qblk"):
        bit = 4
        while bit < lax.axis_size(axis):
            far.append((axis, bit | bit >> 1))
            bit *= 2
    return core, x, y, z, far


def masks_of(chosen):
    order = [0]
    for _, mask in chosen:
        order = order + [o ^ mask for o in order]
    return order


def call(kernel, outs, args, specs, scratch, flops, grant):
    nbytes = sum(math.prod(a.shape) * a.dtype.itemsize for a in (*args, *outs))
    return pl.pallas_call(
        kernel,
        out_shape=outs,
        in_specs=specs,
        out_specs=[pl.BlockSpec(memory_space=pltpu.VMEM)] * len(outs),
        scratch_shapes=scratch,
        compiler_params=pltpu.CompilerParams(vmem_limit_bytes=grant),
        cost_estimate=pl.CostEstimate(flops=flops, bytes_accessed=nbytes, transcendentals=0),
    )(*args)


IN_VMEM = pl.BlockSpec(memory_space=pltpu.VMEM)
IN_SMEM = pl.BlockSpec(memory_space=pltpu.SMEM)


def attention_kernel(cfg, where, query, lens, *refs):
    kv, out_weight = refs[: cfg["blocks"]], refs[cfg["blocks"]]
    send_a, keep_a, send_b, keep_b, stacked, scores, attended, column = refs[cfg["blocks"] + 1 :]
    count = lens.shape[1]
    square = (count, count)
    diagonal = lax.broadcasted_iota(jnp.int32, square, 0) == lax.broadcasted_iota(
        jnp.int32, square, 1
    )
    lens_row = jnp.broadcast_to(lens[...].astype(F32), square)
    column[...] = jnp.sum(jnp.where(diagonal, lens_row, 0.0), axis=1, keepdims=True)
    token_rows, heads, near = cfg["token_rows"], cfg["heads"], cfg["near"]
    head_me, qblk_me = where[0], where[1]
    tile = 2 * near
    keys = kv[0].shape[0]
    factor = HD ** (-0.5) * math.log2(math.e)
    group = max(1, TILE // tile)
    half = out_weight.shape[1] // 2
    for z in (1, 0):
        starts = []
        for o in cfg["order"][z]:
            starts.append(pl.multiple_of((head_me ^ o) * token_rows, token_rows))
        span = jnp.concatenate([column[pl.ds(s, token_rows), :] for s in starts], axis=0)
        span = jnp.concatenate([span] * group, axis=0)
        for first in range(0, heads, group):
            for h in range(group):
                lanes = pl.ds((first + h) * HD, HD)
                for i, s in enumerate(starts):
                    rows = pl.ds(h * tile + i * token_rows, token_rows)
                    stacked[rows, :] = query[pl.ds(s, token_rows), lanes]
            q = stacked[...]
            top = None
            for b in range(cfg["blocks"]):
                s = lax.dot_general(
                    q, kv[b][:, :HD], (((1,), (1,)), ((), ())), preferred_element_type=F32
                )
                base = (qblk_me ^ cfg["offsets"][b]) * keys
                pos = base + lax.broadcasted_iota(jnp.int32, s.shape, 1)
                s = jnp.where(pos.astype(F32) < span, s, -1e30)
                scores[:, b * keys : (b + 1) * keys] = s
                here = jnp.max(s, axis=1, keepdims=True)
                top = here if top is None else jnp.maximum(top, here)
            denom, mixed = 0.0, 0.0
            for b in range(cfg["blocks"]):
                s = scores[:, b * keys : (b + 1) * keys]
                w = jnp.exp2((s - top) * factor)
                denom = denom + jnp.sum(w, axis=1, keepdims=True)
                mixed = mixed + jnp.dot(
                    w.astype(BF16), kv[b][:, HD:], preferred_element_type=F32
                )
            result = (mixed / denom).astype(BF16)
            for h in range(group):
                attended[:, (first + h) * HD : (first + h + 1) * HD] = result[
                    h * tile : (h + 1) * tile
                ]
        a = attended[...]
        for col in range(0, 2 * half, TILE):
            p = jnp.dot(a, out_weight[:, col : col + TILE], preferred_element_type=F32)
            for y in (0, 1):
                rows = p[y * near : (y + 1) * near]
                if col < half:
                    at = slice(col, col + TILE)
                    if z:
                        send_a[y, :, at] = rows.astype(BF16)
                    else:
                        keep_a[y, :, at] = rows
                else:
                    at = slice(col - half, col - half + TILE)
                    if y:
                        send_b[z, :, at] = rows.astype(BF16)
                    else:
                        keep_b[z, :, at] = rows


def attention(where, queries, visible_len, kv, offsets, out_weight, token_rows):
    _, _, y, z, far = links()
    tokens, lanes = queries.shape
    heads = lanes // HD
    far = [link for link in far if link[0] == "head"]
    order = masks_of([*far, y, z])
    blocks = len(order) // 2
    near = blocks // 2 * token_rows
    half = out_weight.shape[1] // 2
    cfg = dict(
        blocks=len(kv),
        token_rows=token_rows,
        heads=heads,
        near=near,
        order=(order[:blocks], order[blocks:]),
        offsets=offsets,
    )
    tile = 2 * near
    rows = max(1, TILE // tile) * tile
    keys = kv[0].shape[0] * len(kv)
    outs = [
        jax.ShapeDtypeStruct((2, near, half), kind) for kind in (BF16, F32, BF16, F32)
    ]
    return call(
        functools.partial(attention_kernel, cfg),
        outs,
        [where, queries, visible_len.reshape(1, tokens), *kv, out_weight],
        [IN_SMEM] + [IN_VMEM] * (3 + len(kv)),
        [
            pltpu.VMEM((rows, HD), BF16),
            pltpu.VMEM((rows, keys), F32),
            pltpu.VMEM((tile, lanes), BF16),
            pltpu.VMEM((tokens, 1), F32),
        ],
        4 * tokens * heads * keys * HD + 2 * tokens * lanes * 2 * half,
        12 * MIB,
    )


def pick_kernel(index, keys, values, own):
    own[:, :HD] = keys[0]
    own[:, HD:] = values[0]


def pick(where, key_cache, value_cache, local_heads):
    rows = key_cache.shape[1]
    group = QH // KVH

    def of_head(i, at):
        return lax.div(at[0] * local_heads, jnp.int32(group)), 0, 0

    block = pl.BlockSpec((1, rows, HD), of_head)
    return pl.pallas_call(
        pick_kernel,
        out_shape=jax.ShapeDtypeStruct((rows, 2 * HD), BF16),
        grid_spec=pltpu.PrefetchScalarGridSpec(
            num_scalar_prefetch=1,
            grid=(1,),
            in_specs=[block, block],
            out_specs=pl.BlockSpec((rows, 2 * HD), lambda i, at: (0, 0)),
        ),
        compiler_params=pltpu.CompilerParams(vmem_limit_bytes=54 * MIB),
        cost_estimate=pl.CostEstimate(flops=COVER, bytes_accessed=8 * rows * HD, transcendentals=0),
    )(where, key_cache, value_cache)


def gather_keys(where, key_cache, value_cache, local_heads):
    own = pick(where, key_cache, value_cache, local_heads)
    core, x, _, _, far = links()
    chosen = [link for link in far if link[0] == "qblk"] + [x, core]
    blocks = [own]
    for link in chosen:
        blocks = blocks + [swap(b, link) for b in blocks]
    return blocks, masks_of(chosen)


def reduce_heads(send_a, keep_a, send_b, keep_b):
    _, _, y, z, far = links()
    got_a, got_b = swap(send_a, z), swap(send_b, y)

    def second(keep, got, link):
        sent = swap((keep[1] + got[1].astype(F32)).astype(BF16), link)
        return keep[0] + got[0].astype(F32) + sent.astype(F32)

    total = jnp.concatenate([second(keep_a, got_a, y), second(keep_b, got_b, z)], axis=1)
    return fold_far(total, [link for link in far if link[0] == "head"])


def fold_far(total, far):
    for link in reversed(far):
        half = total.shape[0] // 2
        total = total[:half] + swap(total[half:].astype(BF16), link).astype(F32)
    return total


def row_cuts(rows):
    units = rows // 8
    first = -(-units // 3)
    return (0, first * 8, 2 * first * 8, rows)


def spread(block, dims, far):
    for link in far:
        block = jnp.concatenate([block, swap(block, link)], axis=0)
    cuts = row_cuts(block.shape[0])
    parts = [block[cuts[i] : cuts[i + 1]][None, None, None] for i in range(3)]
    for stage in range(2):
        got = [swap(parts[i], dims[(i + stage) % 3]) for i in range(3)]
        joined = []
        for i in range(3):
            joined.append(jnp.concatenate([parts[i], got[i]], axis=(i + stage) % 3))
        parts = joined
    parts = [p.reshape(-1, p.shape[-1]) for p in parts]
    return parts, [swap(parts[i], dims[(i + 2) % 3]) for i in range(3)]


def expert_kernel(cfg, where, *refs):
    parts, (gate, up, down), refs = refs[:3], refs[3:6], refs[6:]
    out, hidden = refs
    mine = (where[0] * cfg["blocks"] + where[1]).astype(F32)
    top = cfg["top"]
    total = hidden.shape[0]
    width = out.shape[1]
    sizes = [p.shape[0] for p in parts]
    chunk = cfg["chunk"]

    def run(pieces, at):
        lhs = jnp.concatenate([p[:, :width] for p in pieces], axis=0)
        route = jnp.concatenate([p[:, width:] for p in pieces], axis=0).astype(F32)
        lane = lax.broadcasted_iota(jnp.int32, route.shape, 1)
        hit = (route == mine) & (lane < top)
        weight = sum(pltpu.roll(route, LANES - top * k, 1) for k in (1, 2, 3))
        scale = jnp.sum(jnp.where(hit, weight, 0.0), axis=1, keepdims=True)
        rows = pl.ds(at, lhs.shape[0])
        for f in range(0, hidden.shape[1], TILE):
            g = jnp.dot(lhs, gate[0, :, f : f + TILE], preferred_element_type=F32)
            u = jnp.dot(lhs, up[0, :, f : f + TILE], preferred_element_type=F32)
            hidden[rows, f : f + TILE] = (g / (1.0 + jnp.exp(-g)) * u).astype(BF16)
        h = hidden[rows, :]
        for col in range(0, width, TILE):
            y = jnp.dot(h, down[0, :, col : col + TILE], preferred_element_type=F32) * scale
            out[rows, col : col + TILE] = y.astype(out.dtype)

    if total <= chunk:
        run([p[...] for p in parts], 0)
        return
    at = 0
    for p, size in zip(parts, sizes, strict=True):
        run([p[...]], at)
        at += size


def expert(where, parts, matrices, top, kind):
    width = parts[0].shape[1] - LANES
    rows = sum(p.shape[0] for p in parts)
    hidden = matrices[0].shape[2]
    cfg = dict(blocks=lax.axis_size("qblk"), top=top, chunk=2 * TILE)
    args = [where, *parts, *matrices]
    return call(
        functools.partial(expert_kernel, cfg),
        [jax.ShapeDtypeStruct((rows, width), kind)],
        args,
        [IN_SMEM] + [IN_VMEM] * (len(args) - 1),
        [pltpu.VMEM((rows, hidden), BF16)],
        6 * rows * width * hidden,
        12 * MIB,
    )[0]


def fold(sends, keeps, dims, far):
    keeps = [k.reshape(2, 2, -1, k.shape[-1]) for k in keeps]
    sends = [s.reshape(2, 2, -1, s.shape[-1]) for s in sends]
    got = [swap(sends[i], dims[(i + 2) % 3]) for i in range(3)]
    for stage in (1, 0):
        nxt = []
        for i in range(3):
            axis = (i + stage) % 3
            left = sorted((i + s) % 3 for s in range(stage + 1))
            at = left.index(axis)
            keep = [lax.index_in_dim(keeps[i], k, at, False) for k in (0, 1)]
            new = [lax.index_in_dim(got[i], k, at, False).astype(F32) for k in (0, 1)]
            sent = (keep[1] + new[1]).astype(BF16)
            nxt.append((keep[0] + new[0], swap(sent, dims[axis])))
        keeps, got = [n[0] for n in nxt], [n[1] for n in nxt]
    total = jnp.concatenate([keeps[i] + got[i].astype(F32) for i in range(3)], axis=0)
    return fold_far(total, far)


def norm_kernel(residual, projected, gain, ids, weights, hidden, block):
    total = residual[...].astype(F32) + projected[...]
    mean_square = jnp.mean(total * total, axis=1, keepdims=True)
    hidden[...] = total
    rows, width = total.shape
    block[:, :width] = (total * lax.rsqrt(mean_square + 1e-06) * gain[...]).astype(BF16)
    rest, pieces = weights[...], [ids[...].astype(F32)]
    for _ in range(3):
        piece = rest.astype(BF16).astype(F32)
        pieces.append(piece)
        rest = rest - piece
    used = 4 * ids.shape[0]
    pieces.append(jnp.zeros((LANES - used, rows), F32))
    table = jnp.concatenate(pieces, axis=0).astype(BF16)
    square = (rows, rows)
    diagonal = lax.broadcasted_iota(jnp.int32, square, 0) == lax.broadcasted_iota(
        jnp.int32, square, 1
    )
    eye = jnp.where(diagonal, 1.0, 0.0).astype(BF16)
    turned = lax.dot_general(
        eye, table, (((1,), (1,)), ((), ())), preferred_element_type=F32
    )
    block[:, width:] = turned.astype(BF16)


def norm(residual, projected, gain, expert_ids, route_weights):
    rows, width = residual.shape
    return call(
        norm_kernel,
        [
            jax.ShapeDtypeStruct((rows, width), F32),
            jax.ShapeDtypeStruct((rows, width + LANES), BF16),
        ],
        [residual, projected, gain.reshape(1, width), expert_ids.T, route_weights.T],
        [IN_VMEM] * 5,
        [],
        COVER,
        4 * MIB,
    )


def per_device(
    residual,
    queries,
    key_cache,
    value_cache,
    visible_len,
    out_weight,
    norm_gain,
    expert_ids,
    route_weights,
    w_gate,
    w_up,
    w_down,
):
    core, x, y, z, far = links()
    where = jnp.stack([lax.axis_index("head"), lax.axis_index("qblk")])
    kv, offsets = gather_keys(where, key_cache, value_cache, queries.shape[1] // HD)
    projected = reduce_heads(
        *attention(where, queries, visible_len, kv, offsets, out_weight, residual.shape[0])
    )
    hidden_state, block = norm(residual, projected, norm_gain, expert_ids, route_weights)
    dims = (x, y, z)
    matrices = (w_gate, w_up, w_down)
    own, got = spread(block, dims, far)
    own_c = [swap(p, core) for p in own]
    got_c = [swap(p, core) for p in got]
    top = expert_ids.shape[1]
    back = expert(where, own_c, matrices, top, BF16)
    back = swap(back, core)
    kept = expert(where, own, matrices, top, F32)
    kept = kept + back.astype(F32)
    back = expert(where, got_c, matrices, top, BF16)
    back = swap(back, core)
    sent = expert(where, got, matrices, top, F32)
    sent = (sent + back.astype(F32)).astype(BF16)
    cuts = [0]
    for p in own:
        cuts.append(cuts[-1] + p.shape[0])
    split = [[v[cuts[i] : cuts[i + 1]] for i in range(3)] for v in (sent, kept)]
    mix = fold(*split, dims, far)
    return (hidden_state + mix).astype(BF16)


def solution(mesh):
    in_specs = (
        P(("qblk", "head"), None),
        P("qblk", "head"),
        P(None, "qblk", None),
        P(None, "qblk", None),
        P("qblk"),
        P("head", None),
        P(),
        P(("qblk", "head"), None),
        P(("qblk", "head"), None),
        P(("head", "qblk"), None, None),
        P(("head", "qblk"), None, None),
        P(("head", "qblk"), None, None),
    )
    out_specs = P(("qblk", "head"), None)

    return jax.shard_map(
        per_device, mesh=mesh, in_specs=in_specs, out_specs=out_specs, check_vma=False
    )
```

```python
import functools
import math

import jax
import jax.numpy as jnp
from jax import lax
from jax.experimental import pallas as pl
from jax.experimental.pallas import tpu as pltpu
from jax.sharding import PartitionSpec as P


QH = 32
KVH = 4
HD = 128
F32 = jnp.float32
BF16 = jnp.bfloat16
LANES = 128
TILE = 256
MIB = 1 << 20
COVER = 2 * 10**10


def swap(v, link):
    axis, mask = link
    return lax.ppermute(v, axis, [(i, i ^ mask) for i in range(lax.axis_size(axis))])


def links():
    core, x, y, z = ("qblk", 1), ("qblk", 2), ("head", 1), ("head", 2)
    far = []
    for axis in ("head", "qblk"):
        bit = 4
        while bit < lax.axis_size(axis):
            far.append((axis, bit | bit >> 1))
            bit *= 2
    return core, x, y, z, far


def masks_of(chosen):
    order = [0]
    for _, mask in chosen:
        order = order + [o ^ mask for o in order]
    return order


def call(kernel, outs, args, specs, scratch, flops, grant):
    nbytes = sum(math.prod(a.shape) * a.dtype.itemsize for a in (*args, *outs))
    return pl.pallas_call(
        kernel,
        out_shape=outs,
        in_specs=specs,
        out_specs=[pl.BlockSpec(memory_space=pltpu.VMEM)] * len(outs),
        scratch_shapes=scratch,
        compiler_params=pltpu.CompilerParams(vmem_limit_bytes=grant),
        cost_estimate=pl.CostEstimate(flops=flops, bytes_accessed=nbytes, transcendentals=0),
    )(*args)


IN_VMEM = pl.BlockSpec(memory_space=pltpu.VMEM)


def lens_kernel(lens, column):
    count = lens.shape[1]
    square = (count, count)
    diagonal = lax.broadcasted_iota(jnp.int32, square, 0) == lax.broadcasted_iota(
        jnp.int32, square, 1
    )
    row = jnp.broadcast_to(lens[...].astype(F32), square)
    column[...] = jnp.sum(jnp.where(diagonal, row, 0.0), axis=1, keepdims=True)


def attention_kernel(cfg, query, column, *refs):
    kv, refs = refs[: cfg["blocks"]], refs[cfg["blocks"] :]
    if cfg["z"]:
        out_weight, send_a, send_b, keep_b, stacked, scores, attended = refs
    else:
        out_weight, early_b, keep_a, send_b, keep_b, stacked, scores, attended = refs
        send_b[1] = early_b[...]
    token_rows, heads, near = cfg["token_rows"], cfg["heads"], cfg["near"]
    head_me, qblk_me = lax.axis_index("head"), lax.axis_index("qblk")
    tile = 2 * near
    keys = kv[0].shape[0]
    factor = HD ** (-0.5) * math.log2(math.e)
    group = max(1, TILE // tile)
    starts = []
    for o in cfg["order"]:
        starts.append(pl.multiple_of((head_me ^ o) * token_rows, token_rows))
    span = jnp.concatenate([column[pl.ds(s, token_rows), :] for s in starts], axis=0)
    span = jnp.concatenate([span] * group, axis=0)
    for first in range(0, heads, group):
        for h in range(group):
            lanes = pl.ds((first + h) * HD, HD)
            for i, s in enumerate(starts):
                rows = pl.ds(h * tile + i * token_rows, token_rows)
                stacked[rows, :] = query[pl.ds(s, token_rows), lanes]
        q = stacked[...]
        top = None
        for b in range(cfg["blocks"]):
            s = lax.dot_general(
                q, kv[b][:, :HD], (((1,), (1,)), ((), ())), preferred_element_type=F32
            )
            base = (qblk_me ^ cfg["offsets"][b]) * keys
            pos = base + lax.broadcasted_iota(jnp.int32, s.shape, 1)
            s = jnp.where(pos.astype(F32) < span, s, -1e30)
            scores[:, b * keys : (b + 1) * keys] = s
            here = jnp.max(s, axis=1, keepdims=True)
            top = here if top is None else jnp.maximum(top, here)
        denom, mixed = 0.0, 0.0
        for b in range(cfg["blocks"]):
            s = scores[:, b * keys : (b + 1) * keys]
            w = jnp.exp2((s - top) * factor)
            denom = denom + jnp.sum(w, axis=1, keepdims=True)
            mixed = mixed + jnp.dot(w.astype(BF16), kv[b][:, HD:], preferred_element_type=F32)
        result = (mixed / denom).astype(BF16)
        for h in range(group):
            attended[:, (first + h) * HD : (first + h + 1) * HD] = result[
                h * tile : (h + 1) * tile
            ]
    a = attended[...]
    cut = cfg["cut"]
    for col in range(0, out_weight.shape[1], TILE):
        p = jnp.dot(a, out_weight[:, col : col + TILE], preferred_element_type=F32)
        for y in (0, 1):
            rows = p[y * near : (y + 1) * near]
            if col < cut:
                at = slice(col, col + TILE)
                if cfg["z"]:
                    send_a[y, :, at] = rows.astype(BF16)
                else:
                    keep_a[y, :, at] = rows
                continue
            at = slice(col - cut, col - cut + TILE)
            if not y:
                keep_b[:, at] = rows
            elif cfg["z"]:
                send_b[:, at] = rows.astype(BF16)
            else:
                send_b[0, :, at] = rows.astype(BF16)


def attention(queries, visible_len, kv, offsets, out_weight, token_rows):
    _, _, y, z, far = links()
    tokens, lanes = queries.shape
    heads = lanes // HD
    far = [link for link in far if link[0] == "head"]
    order = masks_of([*far, y, z])
    blocks = len(order) // 2
    near = blocks // 2 * token_rows
    width = out_weight.shape[1]
    cut = -(-5 * width // (8 * TILE)) * TILE
    tile = 2 * near
    rows = max(1, TILE // tile) * tile
    keys = kv[0].shape[0] * len(kv)
    column = call(
        lens_kernel,
        [jax.ShapeDtypeStruct((tokens, 1), F32)],
        [visible_len.reshape(1, tokens)],
        [IN_VMEM],
        [],
        COVER,
        4 * MIB,
    )[0]

    def run(side, outs, more):
        cfg = dict(
            blocks=len(kv),
            token_rows=token_rows,
            heads=heads,
            near=near,
            order=order[side * blocks : (side + 1) * blocks],
            offsets=offsets,
            cut=cut,
            z=side,
        )
        args = [queries, column, *kv, out_weight, *more]
        return call(
            functools.partial(attention_kernel, cfg),
            [jax.ShapeDtypeStruct(shape, kind) for shape, kind in outs],
            args,
            [IN_VMEM] * len(args),
            [
                pltpu.VMEM((rows, HD), BF16),
                pltpu.VMEM((rows, keys), F32),
                pltpu.VMEM((tile, lanes), BF16),
            ],
            2 * tokens * heads * keys * HD + tokens * lanes * width,
            12 * MIB,
        )

    part_a, part_b = (2, near, cut), (near, width - cut)
    send_a, early_b, keep_b1 = run(1, [(part_a, BF16), (part_b, BF16), (part_b, F32)], [])
    got_a = swap(send_a, z)
    keep_a, send_b, keep_b0 = run(
        0, [(part_a, F32), ((2, *part_b), BF16), (part_b, F32)], [early_b]
    )
    got_b = swap(send_b, y)

    def second(keep0, keep1, got, link):
        sent = (keep1 + got[1].astype(F32)).astype(BF16)
        sent = swap(sent, link)
        return keep0 + got[0].astype(F32) + sent.astype(F32)

    total = jnp.concatenate(
        [second(keep_a[0], keep_a[1], got_a, y), second(keep_b0, keep_b1, got_b, z)],
        axis=1,
    )
    return fold_far(total, far)


def gather_keys(key_cache, value_cache, kv_index):
    own = jnp.concatenate(
        [
            lax.dynamic_index_in_dim(key_cache, kv_index, 0, keepdims=False),
            lax.dynamic_index_in_dim(value_cache, kv_index, 0, keepdims=False),
        ],
        axis=1,
    )
    core, x, _, _, far = links()
    chosen = [link for link in far if link[0] == "qblk"] + [x, core]
    blocks = [own]
    for link in chosen:
        blocks = blocks + [swap(b, link) for b in blocks]
    return blocks, masks_of(chosen)


def fold_far(total, far):
    for link in reversed(far):
        half = total.shape[0] // 2
        total = total[:half] + swap(total[half:].astype(BF16), link).astype(F32)
    return total


def row_cuts(rows):
    units = rows // 8
    first = -(-units // 3)
    return (0, first * 8, 2 * first * 8, rows)


def spread(block, dims, far):
    for link in far:
        block = jnp.concatenate([block, swap(block, link)], axis=0)
    cuts = row_cuts(block.shape[0])
    parts = [block[cuts[i] : cuts[i + 1]][None, None, None] for i in range(3)]
    for stage in range(2):
        got = [swap(parts[i], dims[(i + stage) % 3]) for i in range(3)]
        joined = []
        for i in range(3):
            joined.append(jnp.concatenate([parts[i], got[i]], axis=(i + stage) % 3))
        parts = joined
    parts = [p.reshape(-1, p.shape[-1]) for p in parts]
    return parts, [swap(parts[i], dims[(i + 2) % 3]) for i in range(3)]


def expert_kernel(cfg, *refs):
    parts, (gate, up, down), refs = refs[:3], refs[3:6], refs[6:]
    out, hidden = refs
    mine = (lax.axis_index("head") * cfg["blocks"] + lax.axis_index("qblk")).astype(F32)
    top = cfg["top"]
    total = hidden.shape[0]
    width = out.shape[1]
    sizes = [p.shape[0] for p in parts]
    chunk = cfg["chunk"]

    def run(pieces, at):
        lhs = jnp.concatenate([p[:, :width] for p in pieces], axis=0)
        route = jnp.concatenate([p[:, width:] for p in pieces], axis=0).astype(F32)
        lane = lax.broadcasted_iota(jnp.int32, route.shape, 1)
        hit = (route == mine) & (lane < top)
        weight = sum(pltpu.roll(route, LANES - top * k, 1) for k in (1, 2, 3))
        scale = jnp.sum(jnp.where(hit, weight, 0.0), axis=1, keepdims=True)
        rows = pl.ds(at, lhs.shape[0])
        for f in range(0, hidden.shape[1], TILE):
            g = jnp.dot(lhs, gate[0, :, f : f + TILE], preferred_element_type=F32)
            u = jnp.dot(lhs, up[0, :, f : f + TILE], preferred_element_type=F32)
            hidden[rows, f : f + TILE] = (g / (1.0 + jnp.exp(-g)) * u).astype(BF16)
        h = hidden[rows, :]
        for col in range(0, width, TILE):
            y = jnp.dot(h, down[0, :, col : col + TILE], preferred_element_type=F32) * scale
            out[rows, col : col + TILE] = y.astype(out.dtype)

    if total <= chunk:
        run([p[...] for p in parts], 0)
        return
    at = 0
    for p, size in zip(parts, sizes, strict=True):
        run([p[...]], at)
        at += size


def expert(parts, matrices, top, kind):
    width = parts[0].shape[1] - LANES
    rows = sum(p.shape[0] for p in parts)
    hidden = matrices[0].shape[2]
    cfg = dict(blocks=lax.axis_size("qblk"), top=top, chunk=2 * TILE)
    args = [*parts, *matrices]
    return call(
        functools.partial(expert_kernel, cfg),
        [jax.ShapeDtypeStruct((rows, width), kind)],
        args,
        [IN_VMEM] * len(args),
        [pltpu.VMEM((rows, hidden), BF16)],
        6 * rows * width * hidden,
        12 * MIB,
    )[0]


def fold(sends, keeps, dims, far):
    keeps = [k.reshape(2, 2, -1, k.shape[-1]) for k in keeps]
    sends = [s.reshape(2, 2, -1, s.shape[-1]) for s in sends]
    got = [swap(sends[i], dims[(i + 2) % 3]) for i in range(3)]
    for stage in (1, 0):
        nxt = []
        for i in range(3):
            axis = (i + stage) % 3
            left = sorted((i + s) % 3 for s in range(stage + 1))
            at = left.index(axis)
            keep = [lax.index_in_dim(keeps[i], k, at, False) for k in (0, 1)]
            new = [lax.index_in_dim(got[i], k, at, False).astype(F32) for k in (0, 1)]
            sent = (keep[1] + new[1]).astype(BF16)
            nxt.append((keep[0] + new[0], swap(sent, dims[axis])))
        keeps, got = [n[0] for n in nxt], [n[1] for n in nxt]
    total = jnp.concatenate([keeps[i] + got[i].astype(F32) for i in range(3)], axis=0)
    return fold_far(total, far)


def norm_kernel(residual, projected, gain, ids, weights, hidden, block):
    total = residual[...].astype(F32) + projected[...]
    mean_square = jnp.mean(total * total, axis=1, keepdims=True)
    hidden[...] = total
    rows, width = total.shape
    block[:, :width] = (total * lax.rsqrt(mean_square + 1e-06) * gain[...]).astype(BF16)
    rest, pieces = weights[...], [ids[...].astype(F32)]
    for _ in range(3):
        piece = rest.astype(BF16).astype(F32)
        pieces.append(piece)
        rest = rest - piece
    used = 4 * ids.shape[0]
    pieces.append(jnp.zeros((LANES - used, rows), F32))
    table = jnp.concatenate(pieces, axis=0).astype(BF16)
    square = (rows, rows)
    diagonal = lax.broadcasted_iota(jnp.int32, square, 0) == lax.broadcasted_iota(
        jnp.int32, square, 1
    )
    eye = jnp.where(diagonal, 1.0, 0.0).astype(BF16)
    turned = lax.dot_general(
        eye, table, (((1,), (1,)), ((), ())), preferred_element_type=F32
    )
    block[:, width:] = turned.astype(BF16)


def norm(residual, projected, gain, expert_ids, route_weights):
    rows, width = residual.shape
    return call(
        norm_kernel,
        [
            jax.ShapeDtypeStruct((rows, width), F32),
            jax.ShapeDtypeStruct((rows, width + LANES), BF16),
        ],
        [residual, projected, gain.reshape(1, width), expert_ids.T, route_weights.T],
        [IN_VMEM] * 5,
        [],
        COVER,
        4 * MIB,
    )


def per_device(
    residual,
    queries,
    key_cache,
    value_cache,
    visible_len,
    out_weight,
    norm_gain,
    expert_ids,
    route_weights,
    w_gate,
    w_up,
    w_down,
):
    core, x, y, z, far = links()
    local_heads = queries.shape[1] // HD
    kv_index = lax.axis_index("head") * local_heads // (QH // KVH)
    kv, offsets = gather_keys(key_cache, value_cache, kv_index)
    projected = attention(queries, visible_len, kv, offsets, out_weight, residual.shape[0])
    hidden_state, block = norm(residual, projected, norm_gain, expert_ids, route_weights)
    dims = (x, y, z)
    matrices = (w_gate, w_up, w_down)
    own, got = spread(block, dims, far)
    own_c = [swap(p, core) for p in own]
    got_c = [swap(p, core) for p in got]
    top = expert_ids.shape[1]
    back = expert(own_c, matrices, top, BF16)
    back = swap(back, core)
    kept = expert(own, matrices, top, F32)
    kept = kept + back.astype(F32)
    back = expert(got_c, matrices, top, BF16)
    back = swap(back, core)
    sent = expert(got, matrices, top, F32)
    sent = (sent + back.astype(F32)).astype(BF16)
    cuts = [0]
    for p in own:
        cuts.append(cuts[-1] + p.shape[0])
    split = [[v[cuts[i] : cuts[i + 1]] for i in range(3)] for v in (sent, kept)]
    mix = fold(*split, dims, far)
    return (hidden_state + mix).astype(BF16)


def solution(mesh):
    in_specs = (
        P(("qblk", "head"), None),
        P("qblk", "head"),
        P(None, "qblk", None),
        P(None, "qblk", None),
        P("qblk"),
        P("head", None),
        P(),
        P(("qblk", "head"), None),
        P(("qblk", "head"), None),
        P(("head", "qblk"), None, None),
        P(("head", "qblk"), None, None),
        P(("head", "qblk"), None, None),
    )
    out_specs = P(("qblk", "head"), None)

    return jax.shard_map(
        per_device, mesh=mesh, in_specs=in_specs, out_specs=out_specs, check_vma=False
    )
```

```python
import functools
import math

import jax
import jax.numpy as jnp
from jax import lax
from jax.experimental import pallas as pl
from jax.experimental.pallas import tpu as pltpu
from jax.sharding import PartitionSpec as P


QH = 32
KVH = 4
HD = 128
F32 = jnp.float32
BF16 = jnp.bfloat16
LANES = 128
TILE = 256
MIB = 1 << 20
COVER = 2 * 10**10


def swap(v, link):
    axis, mask = link
    return lax.ppermute(v, axis, [(i, i ^ mask) for i in range(lax.axis_size(axis))])


def links():
    core, x, y, z = ("qblk", 1), ("qblk", 2), ("head", 1), ("head", 2)
    far = []
    for axis in ("head", "qblk"):
        bit = 4
        while bit < lax.axis_size(axis):
            far.append((axis, bit | bit >> 1))
            bit *= 2
    return core, x, y, z, far


def masks_of(chosen):
    order = [0]
    for _, mask in chosen:
        order = order + [o ^ mask for o in order]
    return order


def call(kernel, outs, args, specs, scratch, flops, grant):
    nbytes = sum(math.prod(a.shape) * a.dtype.itemsize for a in (*args, *outs))
    return pl.pallas_call(
        kernel,
        out_shape=outs,
        in_specs=specs,
        out_specs=[pl.BlockSpec(memory_space=pltpu.VMEM)] * len(outs),
        scratch_shapes=scratch,
        compiler_params=pltpu.CompilerParams(vmem_limit_bytes=grant),
        cost_estimate=pl.CostEstimate(flops=flops, bytes_accessed=nbytes, transcendentals=0),
    )(*args)


IN_VMEM = pl.BlockSpec(memory_space=pltpu.VMEM)


def spans(first, last):
    return [(at, min(at + TILE, last)) for at in range(first, last, TILE)]


def lens_kernel(lens, column):
    count = lens.shape[1]
    square = (count, count)
    diagonal = lax.broadcasted_iota(jnp.int32, square, 0) == lax.broadcasted_iota(
        jnp.int32, square, 1
    )
    row = jnp.broadcast_to(lens[...].astype(F32), square)
    column[...] = jnp.sum(jnp.where(diagonal, row, 0.0), axis=1, keepdims=True)


def attention_kernel(cfg, query, column, *refs):
    kv, refs = refs[: cfg["blocks"]], refs[cfg["blocks"] :]
    if cfg["z"]:
        out_weight, send_a, send_b, keep_b, stacked, scores, attended = refs
    else:
        out_weight, early_b, keep_a, send_b, keep_b, stacked, scores, attended = refs
        send_b[1] = early_b[...]
    token_rows, heads, near = cfg["token_rows"], cfg["heads"], cfg["near"]
    head_me, qblk_me = lax.axis_index("head"), lax.axis_index("qblk")
    tile = 2 * near
    keys = kv[0].shape[0]
    factor = HD ** (-0.5) * math.log2(math.e)
    group = max(1, TILE // tile)
    starts = []
    for o in cfg["order"]:
        starts.append(pl.multiple_of((head_me ^ o) * token_rows, token_rows))
    span = jnp.concatenate([column[pl.ds(s, token_rows), :] for s in starts], axis=0)
    span = jnp.concatenate([span] * group, axis=0)
    for first in range(0, heads, group):
        for h in range(group):
            lanes = pl.ds((first + h) * HD, HD)
            for i, s in enumerate(starts):
                rows = pl.ds(h * tile + i * token_rows, token_rows)
                stacked[rows, :] = query[pl.ds(s, token_rows), lanes]
        q = stacked[...]
        top = None
        for b in range(cfg["blocks"]):
            s = lax.dot_general(
                q, kv[b][:, :HD], (((1,), (1,)), ((), ())), preferred_element_type=F32
            )
            base = (qblk_me ^ cfg["offsets"][b]) * keys
            pos = base + lax.broadcasted_iota(jnp.int32, s.shape, 1)
            s = jnp.where(pos.astype(F32) < span, s, -1e30)
            scores[:, b * keys : (b + 1) * keys] = s
            here = jnp.max(s, axis=1, keepdims=True)
            top = here if top is None else jnp.maximum(top, here)
        denom, mixed = 0.0, 0.0
        for b in range(cfg["blocks"]):
            s = scores[:, b * keys : (b + 1) * keys]
            w = jnp.exp2((s - top) * factor)
            denom = denom + jnp.sum(w, axis=1, keepdims=True)
            mixed = mixed + jnp.dot(w.astype(BF16), kv[b][:, HD:], preferred_element_type=F32)
        result = (mixed / denom).astype(BF16)
        for h in range(group):
            attended[:, (first + h) * HD : (first + h + 1) * HD] = result[
                h * tile : (h + 1) * tile
            ]
    a = attended[...]
    cut = cfg["cut"]
    for col, end in spans(0, cut) + spans(cut, out_weight.shape[1]):
        p = jnp.dot(a, out_weight[:, col:end], preferred_element_type=F32)
        for y in (0, 1):
            rows = p[y * near : (y + 1) * near]
            if col < cut:
                at = slice(col, end)
                if cfg["z"]:
                    send_a[y, :, at] = rows.astype(BF16)
                else:
                    keep_a[y, :, at] = rows
                continue
            at = slice(col - cut, end - cut)
            if not y:
                keep_b[:, at] = rows
            elif cfg["z"]:
                send_b[:, at] = rows.astype(BF16)
            else:
                send_b[0, :, at] = rows.astype(BF16)


def attention(queries, visible_len, kv, offsets, out_weight, token_rows):
    _, _, y, z, far = links()
    tokens, lanes = queries.shape
    heads = lanes // HD
    far = [link for link in far if link[0] == "head"]
    order = masks_of([*far, y, z])
    blocks = len(order) // 2
    near = blocks // 2 * token_rows
    width = out_weight.shape[1]
    cut = -(-9 * width // (16 * LANES)) * LANES
    tile = 2 * near
    rows = max(1, TILE // tile) * tile
    keys = kv[0].shape[0] * len(kv)
    column = call(
        lens_kernel,
        [jax.ShapeDtypeStruct((tokens, 1), F32)],
        [visible_len.reshape(1, tokens)],
        [IN_VMEM],
        [],
        COVER,
        4 * MIB,
    )[0]

    def run(side, outs, more):
        cfg = dict(
            blocks=len(kv),
            token_rows=token_rows,
            heads=heads,
            near=near,
            order=order[side * blocks : (side + 1) * blocks],
            offsets=offsets,
            cut=cut,
            z=side,
        )
        args = [queries, column, *kv, out_weight, *more]
        return call(
            functools.partial(attention_kernel, cfg),
            [jax.ShapeDtypeStruct(shape, kind) for shape, kind in outs],
            args,
            [IN_VMEM] * len(args),
            [
                pltpu.VMEM((rows, HD), BF16),
                pltpu.VMEM((rows, keys), F32),
                pltpu.VMEM((tile, lanes), BF16),
            ],
            2 * tokens * heads * keys * HD + tokens * lanes * width,
            12 * MIB,
        )

    part_a, part_b = (2, near, cut), (near, width - cut)
    send_a, early_b, keep_b1 = run(1, [(part_a, BF16), (part_b, BF16), (part_b, F32)], [])
    got_a = swap(send_a, z)
    keep_a, send_b, keep_b0 = run(
        0, [(part_a, F32), ((2, *part_b), BF16), (part_b, F32)], [early_b]
    )
    got_b = swap(send_b, y)

    def second(keep0, keep1, got, link):
        sent = (keep1 + got[1].astype(F32)).astype(BF16)
        sent = swap(sent, link)
        return keep0 + got[0].astype(F32) + sent.astype(F32)

    total = jnp.concatenate(
        [second(keep_a[0], keep_a[1], got_a, y), second(keep_b0, keep_b1, got_b, z)],
        axis=1,
    )
    return fold_far(total, far)


def gather_keys(key_cache, value_cache, kv_index):
    own = jnp.concatenate(
        [
            lax.dynamic_index_in_dim(key_cache, kv_index, 0, keepdims=False),
            lax.dynamic_index_in_dim(value_cache, kv_index, 0, keepdims=False),
        ],
        axis=1,
    )
    core, x, _, _, far = links()
    chosen = [link for link in far if link[0] == "qblk"] + [x, core]
    blocks = [own]
    for link in chosen:
        blocks = blocks + [swap(b, link) for b in blocks]
    return blocks, masks_of(chosen)


def fold_far(total, far):
    for link in reversed(far):
        half = total.shape[0] // 2
        total = total[:half] + swap(total[half:].astype(BF16), link).astype(F32)
    return total


def row_cuts(rows):
    units = rows // 8
    first = -(-units // 3)
    return (0, first * 8, 2 * first * 8, rows)


def spread(block, first, dims, far):
    for link in far:
        block = jnp.concatenate([block, swap(block, link)], axis=0)
    cuts = row_cuts(block.shape[0])
    parts = []
    for i in range(3):
        part = block[cuts[i] : cuts[i + 1]]
        if i == 0 and first.shape[0] == cuts[1]:
            part = first
        parts.append(part[None, None, None])
    for stage in range(2):
        got = [swap(parts[i], dims[(i + stage) % 3]) for i in range(3)]
        joined = []
        for i in range(3):
            joined.append(jnp.concatenate([parts[i], got[i]], axis=(i + stage) % 3))
        parts = joined
    parts = [p.reshape(-1, p.shape[-1]) for p in parts]
    return parts, [swap(parts[i], dims[(i + 2) % 3]) for i in range(3)]


def expert_kernel(cfg, *refs):
    parts, (gate, up, down), refs = refs[:3], refs[3:6], refs[6:]
    out, hidden = refs
    mine = (lax.axis_index("head") * cfg["blocks"] + lax.axis_index("qblk")).astype(F32)
    top = cfg["top"]
    total = hidden.shape[0]
    width = out.shape[1]
    sizes = [p.shape[0] for p in parts]
    chunk = cfg["chunk"]

    def run(pieces, at):
        lhs = jnp.concatenate([p[:, :width] for p in pieces], axis=0)
        route = jnp.concatenate([p[:, width:] for p in pieces], axis=0).astype(F32)
        lane = lax.broadcasted_iota(jnp.int32, route.shape, 1)
        hit = (route == mine) & (lane < top)
        weight = sum(pltpu.roll(route, LANES - top * k, 1) for k in (1, 2, 3))
        scale = jnp.sum(jnp.where(hit, weight, 0.0), axis=1, keepdims=True)
        rows = pl.ds(at, lhs.shape[0])
        for f in range(0, hidden.shape[1], TILE):
            g = jnp.dot(lhs, gate[0, :, f : f + TILE], preferred_element_type=F32)
            u = jnp.dot(lhs, up[0, :, f : f + TILE], preferred_element_type=F32)
            hidden[rows, f : f + TILE] = (g / (1.0 + jnp.exp(-g)) * u).astype(BF16)
        h = hidden[rows, :]
        for col in range(0, width, TILE):
            y = jnp.dot(h, down[0, :, col : col + TILE], preferred_element_type=F32) * scale
            out[rows, col : col + TILE] = y.astype(out.dtype)

    if total <= chunk:
        run([p[...] for p in parts], 0)
        return
    at = 0
    for p, size in zip(parts, sizes, strict=True):
        run([p[...]], at)
        at += size


def expert(parts, matrices, top, kind):
    width = parts[0].shape[1] - LANES
    rows = sum(p.shape[0] for p in parts)
    hidden = matrices[0].shape[2]
    cfg = dict(blocks=lax.axis_size("qblk"), top=top, chunk=2 * TILE)
    args = [*parts, *matrices]
    return call(
        functools.partial(expert_kernel, cfg),
        [jax.ShapeDtypeStruct((rows, width), kind)],
        args,
        [IN_VMEM] * len(args),
        [pltpu.VMEM((rows, hidden), BF16)],
        6 * rows * width * hidden,
        12 * MIB,
    )[0]


def fold(sends, keeps, dims, far):
    keeps = [k.reshape(2, 2, -1, k.shape[-1]) for k in keeps]
    sends = [s.reshape(2, 2, -1, s.shape[-1]) for s in sends]
    got = [swap(sends[i], dims[(i + 2) % 3]) for i in range(3)]
    for stage in (1, 0):
        nxt = []
        for i in range(3):
            axis = (i + stage) % 3
            left = sorted((i + s) % 3 for s in range(stage + 1))
            at = left.index(axis)
            keep = [lax.index_in_dim(keeps[i], k, at, False) for k in (0, 1)]
            new = [lax.index_in_dim(got[i], k, at, False).astype(F32) for k in (0, 1)]
            sent = (keep[1] + new[1]).astype(BF16)
            nxt.append((keep[0] + new[0], swap(sent, dims[axis])))
        keeps, got = [n[0] for n in nxt], [n[1] for n in nxt]
    total = jnp.concatenate([keeps[i] + got[i].astype(F32) for i in range(3)], axis=0)
    return fold_far(total, far)


def norm_kernel(residual, projected, gain, ids, weights, hidden, block, first):
    total = residual[...].astype(F32) + projected[...]
    mean_square = jnp.mean(total * total, axis=1, keepdims=True)
    hidden[...] = total
    rows, width = total.shape
    block[:, :width] = (total * lax.rsqrt(mean_square + 1e-06) * gain[...]).astype(BF16)
    rest, pieces = weights[...], [ids[...].astype(F32)]
    for _ in range(3):
        piece = rest.astype(BF16).astype(F32)
        pieces.append(piece)
        rest = rest - piece
    used = 4 * ids.shape[0]
    pieces.append(jnp.zeros((LANES - used, rows), F32))
    table = jnp.concatenate(pieces, axis=0).astype(BF16)
    square = (rows, rows)
    diagonal = lax.broadcasted_iota(jnp.int32, square, 0) == lax.broadcasted_iota(
        jnp.int32, square, 1
    )
    eye = jnp.where(diagonal, 1.0, 0.0).astype(BF16)
    turned = lax.dot_general(
        eye, table, (((1,), (1,)), ((), ())), preferred_element_type=F32
    )
    block[:, width:] = turned.astype(BF16)
    first[...] = block[: first.shape[0], :]


def norm(residual, projected, gain, expert_ids, route_weights, gathered):
    rows, width = residual.shape
    return call(
        norm_kernel,
        [
            jax.ShapeDtypeStruct((rows, width), F32),
            jax.ShapeDtypeStruct((rows, width + LANES), BF16),
            jax.ShapeDtypeStruct((min(rows, row_cuts(gathered)[1]), width + LANES), BF16),
        ],
        [residual, projected, gain.reshape(1, width), expert_ids.T, route_weights.T],
        [IN_VMEM] * 5,
        [],
        COVER,
        4 * MIB,
    )


def per_device(
    residual,
    queries,
    key_cache,
    value_cache,
    visible_len,
    out_weight,
    norm_gain,
    expert_ids,
    route_weights,
    w_gate,
    w_up,
    w_down,
):
    core, x, y, z, far = links()
    local_heads = queries.shape[1] // HD
    kv_index = lax.axis_index("head") * local_heads // (QH // KVH)
    kv, offsets = gather_keys(key_cache, value_cache, kv_index)
    projected = attention(queries, visible_len, kv, offsets, out_weight, residual.shape[0])
    dims = (x, y, z)
    hidden_state, block, first = norm(
        residual, projected, norm_gain, expert_ids, route_weights, residual.shape[0] << len(far)
    )
    matrices = (w_gate, w_up, w_down)
    own, got = spread(block, first, dims, far)
    own_c = [swap(p, core) for p in own]
    got_c = [swap(p, core) for p in got]
    top = expert_ids.shape[1]
    back = expert(own_c, matrices, top, BF16)
    back = swap(back, core)
    kept = expert(own, matrices, top, F32)
    kept = kept + back.astype(F32)
    back = expert(got_c, matrices, top, BF16)
    back = swap(back, core)
    sent = expert(got, matrices, top, F32)
    sent = (sent + back.astype(F32)).astype(BF16)
    cuts = [0]
    for p in own:
        cuts.append(cuts[-1] + p.shape[0])
    split = [[v[cuts[i] : cuts[i + 1]] for i in range(3)] for v in (sent, kept)]
    mix = fold(*split, dims, far)
    return (hidden_state + mix).astype(BF16)


def solution(mesh):
    in_specs = (
        P(("qblk", "head"), None),
        P("qblk", "head"),
        P(None, "qblk", None),
        P(None, "qblk", None),
        P("qblk"),
        P("head", None),
        P(),
        P(("qblk", "head"), None),
        P(("qblk", "head"), None),
        P(("head", "qblk"), None, None),
        P(("head", "qblk"), None, None),
        P(("head", "qblk"), None, None),
    )
    out_specs = P(("qblk", "head"), None)

    return jax.shard_map(
        per_device, mesh=mesh, in_specs=in_specs, out_specs=out_specs, check_vma=False
    )
```

```python
import functools
import math

import jax
import jax.numpy as jnp
from jax import lax
from jax.experimental import pallas as pl
from jax.experimental.pallas import tpu as pltpu
from jax.sharding import PartitionSpec as P


QH = 32
KVH = 4
HD = 128
F32 = jnp.float32
BF16 = jnp.bfloat16
LANES = 128
TILE = 256
MIB = 1 << 20
COVER = 2 * 10**10


def swap(v, link):
    axis, mask = link
    return lax.ppermute(v, axis, [(i, i ^ mask) for i in range(lax.axis_size(axis))])


def links():
    core, x, y, z = ("qblk", 1), ("qblk", 2), ("head", 1), ("head", 2)
    far = []
    for axis in ("head", "qblk"):
        bit = 4
        while bit < lax.axis_size(axis):
            far.append((axis, bit | bit >> 1))
            bit *= 2
    return core, x, y, z, far


def masks_of(chosen):
    order = [0]
    for _, mask in chosen:
        order = order + [o ^ mask for o in order]
    return order


def call(kernel, outs, args, specs, scratch, flops, grant):
    nbytes = sum(math.prod(a.shape) * a.dtype.itemsize for a in (*args, *outs))
    return pl.pallas_call(
        kernel,
        out_shape=outs,
        in_specs=specs,
        out_specs=[pl.BlockSpec(memory_space=pltpu.VMEM)] * len(outs),
        scratch_shapes=scratch,
        compiler_params=pltpu.CompilerParams(vmem_limit_bytes=grant),
        cost_estimate=pl.CostEstimate(flops=flops, bytes_accessed=nbytes, transcendentals=0),
    )(*args)


IN_VMEM = pl.BlockSpec(memory_space=pltpu.VMEM)


def spans(first, last):
    return [(at, min(at + TILE, last)) for at in range(first, last, TILE)]


def lens_kernel(lens, column):
    count = lens.shape[1]
    square = (count, count)
    diagonal = lax.broadcasted_iota(jnp.int32, square, 0) == lax.broadcasted_iota(
        jnp.int32, square, 1
    )
    row = jnp.broadcast_to(lens[...].astype(F32), square)
    column[...] = jnp.sum(jnp.where(diagonal, row, 0.0), axis=1, keepdims=True)


def attention_kernel(cfg, query, column, *refs):
    kv, refs = refs[: cfg["blocks"]], refs[cfg["blocks"] :]
    if cfg["z"]:
        out_weight, send_a, send_b, keep_b, stacked, scores, attended = refs
    else:
        out_weight, early_b, keep_a, send_b, keep_b, stacked, scores, attended = refs
        send_b[1] = early_b[...]
    token_rows, heads, near = cfg["token_rows"], cfg["heads"], cfg["near"]
    head_me, qblk_me = lax.axis_index("head"), lax.axis_index("qblk")
    tile = 2 * near
    keys = kv[0].shape[0]
    factor = HD ** (-0.5) * math.log2(math.e)
    group = max(1, TILE // tile)
    starts = []
    for o in cfg["order"]:
        starts.append(pl.multiple_of((head_me ^ o) * token_rows, token_rows))
    span = jnp.concatenate([column[pl.ds(s, token_rows), :] for s in starts], axis=0)
    span = jnp.concatenate([span] * group, axis=0)
    for first in range(0, heads, group):
        for h in range(group):
            lanes = pl.ds((first + h) * HD, HD)
            for i, s in enumerate(starts):
                rows = pl.ds(h * tile + i * token_rows, token_rows)
                stacked[rows, :] = query[pl.ds(s, token_rows), lanes]
        q = stacked[...]
        top = None
        for b in range(cfg["blocks"]):
            s = lax.dot_general(
                q, kv[b][:, :HD], (((1,), (1,)), ((), ())), preferred_element_type=F32
            )
            base = (qblk_me ^ cfg["offsets"][b]) * keys
            pos = base + lax.broadcasted_iota(jnp.int32, s.shape, 1)
            s = jnp.where(pos.astype(F32) < span, s, -1e30)
            scores[:, b * keys : (b + 1) * keys] = s
            here = jnp.max(s, axis=1, keepdims=True)
            top = here if top is None else jnp.maximum(top, here)
        denom, mixed = 0.0, 0.0
        for b in range(cfg["blocks"]):
            s = scores[:, b * keys : (b + 1) * keys]
            w = jnp.exp2((s - top) * factor)
            denom = denom + jnp.sum(w, axis=1, keepdims=True)
            mixed = mixed + jnp.dot(w.astype(BF16), kv[b][:, HD:], preferred_element_type=F32)
        result = (mixed / denom).astype(BF16)
        for h in range(group):
            attended[:, (first + h) * HD : (first + h + 1) * HD] = result[
                h * tile : (h + 1) * tile
            ]
    a = attended[...]
    cut = cfg["cut"]
    for col, end in spans(0, cut) + spans(cut, out_weight.shape[1]):
        p = jnp.dot(a, out_weight[:, col:end], preferred_element_type=F32)
        for y in (0, 1):
            rows = p[y * near : (y + 1) * near]
            if col < cut:
                at = slice(col, end)
                if cfg["z"]:
                    send_a[y, :, at] = rows.astype(BF16)
                else:
                    keep_a[y, :, at] = rows
                continue
            at = slice(col - cut, end - cut)
            if not y:
                keep_b[:, at] = rows
            elif cfg["z"]:
                send_b[:, at] = rows.astype(BF16)
            else:
                send_b[0, :, at] = rows.astype(BF16)


def attention(queries, visible_len, kv, offsets, out_weight, token_rows):
    _, _, y, z, far = links()
    tokens, lanes = queries.shape
    heads = lanes // HD
    far = [link for link in far if link[0] == "head"]
    order = masks_of([*far, y, z])
    blocks = len(order) // 2
    near = blocks // 2 * token_rows
    width = out_weight.shape[1]
    cut = -(-9 * width // (16 * LANES)) * LANES
    tile = 2 * near
    rows = max(1, TILE // tile) * tile
    keys = kv[0].shape[0] * len(kv)
    column = call(
        lens_kernel,
        [jax.ShapeDtypeStruct((tokens, 1), F32)],
        [visible_len.reshape(1, tokens)],
        [IN_VMEM],
        [],
        COVER,
        4 * MIB,
    )[0]

    def run(side, outs, more):
        cfg = dict(
            blocks=len(kv),
            token_rows=token_rows,
            heads=heads,
            near=near,
            order=order[side * blocks : (side + 1) * blocks],
            offsets=offsets,
            cut=cut,
            z=side,
        )
        args = [queries, column, *kv, out_weight, *more]
        return call(
            functools.partial(attention_kernel, cfg),
            [jax.ShapeDtypeStruct(shape, kind) for shape, kind in outs],
            args,
            [IN_VMEM] * len(args),
            [
                pltpu.VMEM((rows, HD), BF16),
                pltpu.VMEM((rows, keys), F32),
                pltpu.VMEM((tile, lanes), BF16),
            ],
            2 * tokens * heads * keys * HD + tokens * lanes * width,
            12 * MIB,
        )

    part_a, part_b = (2, near, cut), (near, width - cut)
    send_a, early_b, keep_b1 = run(1, [(part_a, BF16), (part_b, BF16), (part_b, F32)], [])
    got_a = swap(send_a, z)
    keep_a, send_b, keep_b0 = run(
        0, [(part_a, F32), ((2, *part_b), BF16), (part_b, F32)], [early_b]
    )
    got_b = swap(send_b, y)

    def second(keep0, keep1, got, link):
        sent = (keep1 + got[1].astype(F32)).astype(BF16)
        sent = swap(sent, link)
        return keep0 + got[0].astype(F32) + sent.astype(F32)

    total = jnp.concatenate(
        [second(keep_a[0], keep_a[1], got_a, y), second(keep_b0, keep_b1, got_b, z)],
        axis=1,
    )
    return fold_far(total, far)


def gather_keys(key_cache, value_cache, kv_index):
    own = jnp.concatenate(
        [
            lax.dynamic_index_in_dim(key_cache, kv_index, 0, keepdims=False),
            lax.dynamic_index_in_dim(value_cache, kv_index, 0, keepdims=False),
        ],
        axis=1,
    )
    core, x, _, _, far = links()
    chosen = [link for link in far if link[0] == "qblk"] + [x, core]
    blocks = [own]
    for link in chosen:
        blocks = blocks + [swap(b, link) for b in blocks]
    return blocks, masks_of(chosen)


def fold_far(total, far):
    for link in reversed(far):
        half = total.shape[0] // 2
        total = total[:half] + swap(total[half:].astype(BF16), link).astype(F32)
    return total


def row_cuts(rows):
    units = rows // 8
    first = -(-units // 3)
    return (0, first * 8, 2 * first * 8, rows)


def spread(block, first, dims, far):
    for link in far:
        block = jnp.concatenate([block, swap(block, link)], axis=0)
    cuts = row_cuts(block.shape[0])
    parts = []
    for i in range(3):
        part = block[cuts[i] : cuts[i + 1]]
        if i == 0 and first.shape[0] == cuts[1]:
            part = first
        parts.append(part[None, None, None])
    for stage in range(2):
        got = [swap(parts[i], dims[(i + stage) % 3]) for i in range(3)]
        joined = []
        for i in range(3):
            joined.append(jnp.concatenate([parts[i], got[i]], axis=(i + stage) % 3))
        parts = joined
    parts = [p.reshape(-1, p.shape[-1]) for p in parts]
    return parts, [swap(parts[i], dims[(i + 2) % 3]) for i in range(3)]


def expert_kernel(cfg, *refs):
    count = cfg["parts"]
    parts, (gate, up, down), refs = refs[:count], refs[count : count + 3], refs[count + 3 :]
    out, hidden = refs
    mine = (lax.axis_index("head") * cfg["blocks"] + lax.axis_index("qblk")).astype(F32)
    top = cfg["top"]
    total = hidden.shape[0]
    width = out.shape[1]
    sizes = [p.shape[0] for p in parts]
    chunk = cfg["chunk"]

    def run(pieces, at):
        lhs = jnp.concatenate([p[:, :width] for p in pieces], axis=0)
        route = jnp.concatenate([p[:, width:] for p in pieces], axis=0).astype(F32)
        lane = lax.broadcasted_iota(jnp.int32, route.shape, 1)
        hit = (route == mine) & (lane < top)
        weight = sum(pltpu.roll(route, LANES - top * k, 1) for k in (1, 2, 3))
        scale = jnp.sum(jnp.where(hit, weight, 0.0), axis=1, keepdims=True)
        rows = pl.ds(at, lhs.shape[0])
        for f in range(0, hidden.shape[1], TILE):
            g = jnp.dot(lhs, gate[0, :, f : f + TILE], preferred_element_type=F32)
            u = jnp.dot(lhs, up[0, :, f : f + TILE], preferred_element_type=F32)
            hidden[rows, f : f + TILE] = (g / (1.0 + jnp.exp(-g)) * u).astype(BF16)
        h = hidden[rows, :]
        for col in range(0, width, TILE):
            y = jnp.dot(h, down[0, :, col : col + TILE], preferred_element_type=F32) * scale
            out[rows, col : col + TILE] = y.astype(out.dtype)

    if total <= chunk:
        run([p[...] for p in parts], 0)
        return
    at = 0
    for p, size in zip(parts, sizes, strict=True):
        run([p[...]], at)
        at += size


def expert(parts, matrices, top, kind):
    width = parts[0].shape[1] - LANES
    rows = sum(p.shape[0] for p in parts)
    hidden = matrices[0].shape[2]
    cfg = dict(blocks=lax.axis_size("qblk"), top=top, chunk=2 * TILE, parts=len(parts))
    args = [*parts, *matrices]
    return call(
        functools.partial(expert_kernel, cfg),
        [jax.ShapeDtypeStruct((rows, width), kind)],
        args,
        [IN_VMEM] * len(args),
        [pltpu.VMEM((rows, hidden), BF16)],
        6 * rows * width * hidden,
        12 * MIB,
    )[0]


def fold(sends, keeps, dims, far):
    keeps = [k.reshape(2, 2, -1, k.shape[-1]) for k in keeps]
    sends = [s.reshape(2, 2, -1, s.shape[-1]) for s in sends]
    got = [swap(sends[i], dims[(i + 2) % 3]) for i in range(3)]
    for stage in (1, 0):
        nxt = []
        for i in range(3):
            axis = (i + stage) % 3
            left = sorted((i + s) % 3 for s in range(stage + 1))
            at = left.index(axis)
            keep = [lax.index_in_dim(keeps[i], k, at, False) for k in (0, 1)]
            new = [lax.index_in_dim(got[i], k, at, False).astype(F32) for k in (0, 1)]
            sent = (keep[1] + new[1]).astype(BF16)
            nxt.append((keep[0] + new[0], swap(sent, dims[axis])))
        keeps, got = [n[0] for n in nxt], [n[1] for n in nxt]
    total = jnp.concatenate([keeps[i] + got[i].astype(F32) for i in range(3)], axis=0)
    return fold_far(total, far)


def norm_kernel(residual, projected, gain, ids, weights, hidden, block, first):
    total = residual[...].astype(F32) + projected[...]
    mean_square = jnp.mean(total * total, axis=1, keepdims=True)
    hidden[...] = total
    rows, width = total.shape
    block[:, :width] = (total * lax.rsqrt(mean_square + 1e-06) * gain[...]).astype(BF16)
    rest, pieces = weights[...], [ids[...].astype(F32)]
    for _ in range(3):
        piece = rest.astype(BF16).astype(F32)
        pieces.append(piece)
        rest = rest - piece
    used = 4 * ids.shape[0]
    pieces.append(jnp.zeros((LANES - used, rows), F32))
    table = jnp.concatenate(pieces, axis=0).astype(BF16)
    square = (rows, rows)
    diagonal = lax.broadcasted_iota(jnp.int32, square, 0) == lax.broadcasted_iota(
        jnp.int32, square, 1
    )
    eye = jnp.where(diagonal, 1.0, 0.0).astype(BF16)
    turned = lax.dot_general(
        eye, table, (((1,), (1,)), ((), ())), preferred_element_type=F32
    )
    block[:, width:] = turned.astype(BF16)
    first[...] = block[: first.shape[0], :]


def norm(residual, projected, gain, expert_ids, route_weights, gathered):
    rows, width = residual.shape
    return call(
        norm_kernel,
        [
            jax.ShapeDtypeStruct((rows, width), F32),
            jax.ShapeDtypeStruct((rows, width + LANES), BF16),
            jax.ShapeDtypeStruct((min(rows, row_cuts(gathered)[1]), width + LANES), BF16),
        ],
        [residual, projected, gain.reshape(1, width), expert_ids.T, route_weights.T],
        [IN_VMEM] * 5,
        [],
        COVER,
        4 * MIB,
    )


def per_device(
    residual,
    queries,
    key_cache,
    value_cache,
    visible_len,
    out_weight,
    norm_gain,
    expert_ids,
    route_weights,
    w_gate,
    w_up,
    w_down,
):
    core, x, y, z, far = links()
    local_heads = queries.shape[1] // HD
    kv_index = lax.axis_index("head") * local_heads // (QH // KVH)
    kv, offsets = gather_keys(key_cache, value_cache, kv_index)
    projected = attention(queries, visible_len, kv, offsets, out_weight, residual.shape[0])
    dims = (x, y, z)
    hidden_state, block, first = norm(
        residual, projected, norm_gain, expert_ids, route_weights, residual.shape[0] << len(far)
    )
    matrices = (w_gate, w_up, w_down)
    own, got = spread(block, first, dims, far)
    own_c = [swap(p, core) for p in own]
    got_c = [swap(p, core) for p in got]
    top = expert_ids.shape[1]

    def run(parts, kind):
        return expert(parts, matrices, top, kind)

    def cut_up(value, parts):
        pieces, at = [], 0
        for p in parts:
            pieces.append(value[at : at + p.shape[0]])
            at += p.shape[0]
        return pieces

    back = swap(run(own_c, BF16), core)
    mine = cut_up(run(own, F32), own)
    kept = [m + b.astype(F32) for m, b in zip(mine, cut_up(back, own), strict=True)]
    sent = []
    for which in (slice(0, 1), slice(1, 3)):
        mine = run(got[which], F32)
        back = swap(run(got_c[which], BF16), core)
        sent += cut_up((mine + back.astype(F32)).astype(BF16), got[which])
    split = (sent, kept)
    mix = fold(*split, dims, far)
    return (hidden_state + mix).astype(BF16)


def solution(mesh):
    in_specs = (
        P(("qblk", "head"), None),
        P("qblk", "head"),
        P(None, "qblk", None),
        P(None, "qblk", None),
        P("qblk"),
        P("head", None),
        P(),
        P(("qblk", "head"), None),
        P(("qblk", "head"), None),
        P(("head", "qblk"), None, None),
        P(("head", "qblk"), None, None),
        P(("head", "qblk"), None, None),
    )
    out_specs = P(("qblk", "head"), None)

    return jax.shard_map(
        per_device, mesh=mesh, in_specs=in_specs, out_specs=out_specs, check_vma=False
    )
```

```python
import functools
import math

import jax
import jax.numpy as jnp
from jax import lax
from jax.experimental import pallas as pl
from jax.experimental.pallas import tpu as pltpu
from jax.sharding import PartitionSpec as P


QH = 32
KVH = 4
HD = 128
F32 = jnp.float32
BF16 = jnp.bfloat16
LANES = 128
TILE = 256
MIB = 1 << 20
COVER = 2 * 10**10


def swap(v, link):
    axis, mask = link
    return lax.ppermute(v, axis, [(i, i ^ mask) for i in range(lax.axis_size(axis))])


def links():
    core, x, y, z = ("qblk", 1), ("qblk", 2), ("head", 1), ("head", 2)
    far = []
    for axis in ("head", "qblk"):
        bit = 4
        while bit < lax.axis_size(axis):
            far.append((axis, bit | bit >> 1))
            bit *= 2
    return core, x, y, z, far


def masks_of(chosen):
    order = [0]
    for _, mask in chosen:
        order = order + [o ^ mask for o in order]
    return order


def call(kernel, outs, args, specs, scratch, flops, grant):
    nbytes = sum(math.prod(a.shape) * a.dtype.itemsize for a in (*args, *outs))
    return pl.pallas_call(
        kernel,
        out_shape=outs,
        in_specs=specs,
        out_specs=[pl.BlockSpec(memory_space=pltpu.VMEM)] * len(outs),
        scratch_shapes=scratch,
        compiler_params=pltpu.CompilerParams(vmem_limit_bytes=grant),
        cost_estimate=pl.CostEstimate(flops=flops, bytes_accessed=nbytes, transcendentals=0),
    )(*args)


IN_VMEM = pl.BlockSpec(memory_space=pltpu.VMEM)


def spans(first, last):
    return [(at, min(at + TILE, last)) for at in range(first, last, TILE)]


def lens_kernel(lens, column):
    count = lens.shape[1]
    square = (count, count)
    diagonal = lax.broadcasted_iota(jnp.int32, square, 0) == lax.broadcasted_iota(
        jnp.int32, square, 1
    )
    row = jnp.broadcast_to(lens[...].astype(F32), square)
    column[...] = jnp.sum(jnp.where(diagonal, row, 0.0), axis=1, keepdims=True)


def attention_kernel(cfg, query, column, *refs):
    kv, refs = refs[: cfg["blocks"]], refs[cfg["blocks"] :]
    if cfg["z"]:
        out_weight, send_a, send_b, keep_b, stacked, scores, attended = refs
    else:
        out_weight, early_b, keep_a, send_b, keep_b, stacked, scores, attended = refs
        send_b[1] = early_b[...]
    token_rows, heads, near = cfg["token_rows"], cfg["heads"], cfg["near"]
    head_me, qblk_me = lax.axis_index("head"), lax.axis_index("qblk")
    tile = 2 * near
    keys = kv[0].shape[0]
    factor = HD ** (-0.5) * math.log2(math.e)
    group = max(1, TILE // tile)
    starts = []
    for o in cfg["order"]:
        starts.append(pl.multiple_of((head_me ^ o) * token_rows, token_rows))
    span = jnp.concatenate([column[pl.ds(s, token_rows), :] for s in starts], axis=0)
    span = jnp.concatenate([span] * group, axis=0)
    for first in range(0, heads, group):
        for h in range(group):
            lanes = pl.ds((first + h) * HD, HD)
            for i, s in enumerate(starts):
                rows = pl.ds(h * tile + i * token_rows, token_rows)
                stacked[rows, :] = query[pl.ds(s, token_rows), lanes]
        q = stacked[...]
        top = None
        for b in range(cfg["blocks"]):
            s = lax.dot_general(
                q, kv[b][:, :HD], (((1,), (1,)), ((), ())), preferred_element_type=F32
            )
            base = (qblk_me ^ cfg["offsets"][b]) * keys
            pos = base + lax.broadcasted_iota(jnp.int32, s.shape, 1)
            s = jnp.where(pos.astype(F32) < span, s, -1e30)
            scores[:, b * keys : (b + 1) * keys] = s
            here = jnp.max(s, axis=1, keepdims=True)
            top = here if top is None else jnp.maximum(top, here)
        denom, mixed = 0.0, 0.0
        for b in range(cfg["blocks"]):
            s = scores[:, b * keys : (b + 1) * keys]
            w = jnp.exp2((s - top) * factor)
            denom = denom + jnp.sum(w, axis=1, keepdims=True)
            mixed = mixed + jnp.dot(w.astype(BF16), kv[b][:, HD:], preferred_element_type=F32)
        result = (mixed / denom).astype(BF16)
        for h in range(group):
            attended[:, (first + h) * HD : (first + h + 1) * HD] = result[
                h * tile : (h + 1) * tile
            ]
    a = attended[...]
    cut = cfg["cut"]
    for col, end in spans(0, cut) + spans(cut, out_weight.shape[1]):
        p = jnp.dot(a, out_weight[:, col:end], preferred_element_type=F32)
        for y in (0, 1):
            rows = p[y * near : (y + 1) * near]
            if col < cut:
                at = slice(col, end)
                if cfg["z"]:
                    send_a[y, :, at] = rows.astype(BF16)
                else:
                    keep_a[y, :, at] = rows
                continue
            at = slice(col - cut, end - cut)
            if not y:
                keep_b[:, at] = rows
            elif cfg["z"]:
                send_b[:, at] = rows.astype(BF16)
            else:
                send_b[0, :, at] = rows.astype(BF16)


def attention(queries, visible_len, kv, offsets, out_weight, token_rows):
    _, _, y, z, far = links()
    tokens, lanes = queries.shape
    heads = lanes // HD
    far = [link for link in far if link[0] == "head"]
    order = masks_of([*far, y, z])
    blocks = len(order) // 2
    near = blocks // 2 * token_rows
    width = out_weight.shape[1]
    cut = -(-9 * width // (16 * LANES)) * LANES
    tile = 2 * near
    rows = max(1, TILE // tile) * tile
    keys = kv[0].shape[0] * len(kv)
    column = call(
        lens_kernel,
        [jax.ShapeDtypeStruct((tokens, 1), F32)],
        [visible_len.reshape(1, tokens)],
        [IN_VMEM],
        [],
        COVER,
        4 * MIB,
    )[0]

    def run(side, outs, more):
        cfg = dict(
            blocks=len(kv),
            token_rows=token_rows,
            heads=heads,
            near=near,
            order=order[side * blocks : (side + 1) * blocks],
            offsets=offsets,
            cut=cut,
            z=side,
        )
        args = [queries, column, *kv, out_weight, *more]
        return call(
            functools.partial(attention_kernel, cfg),
            [jax.ShapeDtypeStruct(shape, kind) for shape, kind in outs],
            args,
            [IN_VMEM] * len(args),
            [
                pltpu.VMEM((rows, HD), BF16),
                pltpu.VMEM((rows, keys), F32),
                pltpu.VMEM((tile, lanes), BF16),
            ],
            2 * tokens * heads * keys * HD + tokens * lanes * width,
            12 * MIB,
        )

    part_a, part_b = (2, near, cut), (near, width - cut)
    send_a, early_b, keep_b1 = run(1, [(part_a, BF16), (part_b, BF16), (part_b, F32)], [])
    got_a = swap(send_a, z)
    keep_a, send_b, keep_b0 = run(
        0, [(part_a, F32), ((2, *part_b), BF16), (part_b, F32)], [early_b]
    )
    got_b = swap(send_b, y)

    def second(keep0, keep1, got, link):
        sent = (keep1 + got[1].astype(F32)).astype(BF16)
        sent = swap(sent, link)
        return keep0 + got[0].astype(F32) + sent.astype(F32)

    total = jnp.concatenate(
        [second(keep_a[0], keep_a[1], got_a, y), second(keep_b0, keep_b1, got_b, z)],
        axis=1,
    )
    return fold_far(total, far)


def gather_keys(key_cache, value_cache, kv_index):
    own = jnp.concatenate(
        [
            lax.dynamic_index_in_dim(key_cache, kv_index, 0, keepdims=False),
            lax.dynamic_index_in_dim(value_cache, kv_index, 0, keepdims=False),
        ],
        axis=1,
    )
    core, x, _, _, far = links()
    chosen = [link for link in far if link[0] == "qblk"] + [x, core]
    blocks = [own]
    for link in chosen:
        blocks = blocks + [swap(b, link) for b in blocks]
    return blocks, masks_of(chosen)


def fold_far(total, far):
    for link in reversed(far):
        half = total.shape[0] // 2
        total = total[:half] + swap(total[half:].astype(BF16), link).astype(F32)
    return total


SUM_WAYS = ((0, 1, 2), (2, 1, 0), (0, 2, 1))


def row_cuts(rows):
    units = rows // 8
    first = -(-units // 3)
    return (0, first * 8, 2 * first * 8, rows)


def spread(block, first, dims, far):
    for link in far:
        block = jnp.concatenate([block, swap(block, link)], axis=0)
    cuts = row_cuts(block.shape[0])
    parts = []
    for i in range(3):
        part = block[cuts[i] : cuts[i + 1]]
        if i == 0 and first.shape[0] == cuts[1]:
            part = first
        parts.append(part[None, None, None])
    for stage in range(2):
        got = [swap(parts[i], dims[(i + stage) % 3]) for i in range(3)]
        joined = []
        for i in range(3):
            joined.append(jnp.concatenate([parts[i], got[i]], axis=(i + stage) % 3))
        parts = joined
    parts = [p.reshape(-1, p.shape[-1]) for p in parts]
    return parts, [swap(parts[i], dims[(i + 2) % 3]) for i in range(3)]


def expert_kernel(cfg, *refs):
    count = cfg["parts"]
    parts, (gate, up, down), refs = refs[:count], refs[count : count + 3], refs[count + 3 :]
    out, hidden = refs
    mine = (lax.axis_index("head") * cfg["blocks"] + lax.axis_index("qblk")).astype(F32)
    top = cfg["top"]
    total = hidden.shape[0]
    width = out.shape[1]
    sizes = [p.shape[0] for p in parts]
    chunk = cfg["chunk"]

    def run(pieces, at):
        lhs = jnp.concatenate([p[:, :width] for p in pieces], axis=0)
        route = jnp.concatenate([p[:, width:] for p in pieces], axis=0).astype(F32)
        lane = lax.broadcasted_iota(jnp.int32, route.shape, 1)
        hit = (route == mine) & (lane < top)
        weight = sum(pltpu.roll(route, LANES - top * k, 1) for k in (1, 2, 3))
        scale = jnp.sum(jnp.where(hit, weight, 0.0), axis=1, keepdims=True)
        rows = pl.ds(at, lhs.shape[0])
        for f in range(0, hidden.shape[1], TILE):
            g = jnp.dot(lhs, gate[0, :, f : f + TILE], preferred_element_type=F32)
            u = jnp.dot(lhs, up[0, :, f : f + TILE], preferred_element_type=F32)
            hidden[rows, f : f + TILE] = (g / (1.0 + jnp.exp(-g)) * u).astype(BF16)
        h = hidden[rows, :]
        for col in range(0, width, TILE):
            y = jnp.dot(h, down[0, :, col : col + TILE], preferred_element_type=F32) * scale
            out[rows, col : col + TILE] = y.astype(out.dtype)

    if total <= chunk:
        run([p[...] for p in parts], 0)
        return
    at = 0
    for p, size in zip(parts, sizes, strict=True):
        run([p[...]], at)
        at += size


def expert(parts, matrices, top, kind):
    width = parts[0].shape[1] - LANES
    rows = sum(p.shape[0] for p in parts)
    hidden = matrices[0].shape[2]
    cfg = dict(blocks=lax.axis_size("qblk"), top=top, chunk=2 * TILE, parts=len(parts))
    args = [*parts, *matrices]
    return call(
        functools.partial(expert_kernel, cfg),
        [jax.ShapeDtypeStruct((rows, width), kind)],
        args,
        [IN_VMEM] * len(args),
        [pltpu.VMEM((rows, hidden), BF16)],
        6 * rows * width * hidden,
        12 * MIB,
    )[0]


def fold(sends, keeps, dims, far):
    sizes = [k.shape[0] // 4 for k in keeps]
    half = sum(sizes) // 2
    pieces, at = [], 0
    for i, size in enumerate(sizes):
        ends = [0, half - at, size] if 0 < half - at < size else [0, size]
        pieces += [(i, a, b) for a, b in zip(ends[:-1], ends[1:], strict=True)]
        at += size

    def cut(values):
        blocks = [v.reshape(2, 2, -1, v.shape[-1]) for v in values]
        return [blocks[i][:, :, a:b] for i, a, b in pieces]

    keeps, sends = cut(keeps), cut(sends)
    ways = [SUM_WAYS[i] for i, _, _ in pieces]
    got = [swap(s, dims[w[2]]) for s, w in zip(sends, ways, strict=True)]
    for stage in (1, 0):
        nxt = []
        for j, way in enumerate(ways):
            axis = way[stage]
            at = sorted(way[: stage + 1]).index(axis)
            keep = [lax.index_in_dim(keeps[j], k, at, False) for k in (0, 1)]
            new = [lax.index_in_dim(got[j], k, at, False).astype(F32) for k in (0, 1)]
            sent = (keep[1] + new[1]).astype(BF16)
            nxt.append((keep[0] + new[0], swap(sent, dims[axis])))
        keeps, got = [n[0] for n in nxt], [n[1] for n in nxt]
    total = jnp.concatenate([k + g.astype(F32) for k, g in zip(keeps, got, strict=True)], axis=0)
    return fold_far(total, far)


def norm_kernel(residual, projected, gain, ids, weights, hidden, block, first):
    total = residual[...].astype(F32) + projected[...]
    mean_square = jnp.mean(total * total, axis=1, keepdims=True)
    hidden[...] = total
    rows, width = total.shape
    block[:, :width] = (total * lax.rsqrt(mean_square + 1e-06) * gain[...]).astype(BF16)
    rest, pieces = weights[...], [ids[...].astype(F32)]
    for _ in range(3):
        piece = rest.astype(BF16).astype(F32)
        pieces.append(piece)
        rest = rest - piece
    used = 4 * ids.shape[0]
    pieces.append(jnp.zeros((LANES - used, rows), F32))
    table = jnp.concatenate(pieces, axis=0).astype(BF16)
    square = (rows, rows)
    diagonal = lax.broadcasted_iota(jnp.int32, square, 0) == lax.broadcasted_iota(
        jnp.int32, square, 1
    )
    eye = jnp.where(diagonal, 1.0, 0.0).astype(BF16)
    turned = lax.dot_general(
        eye, table, (((1,), (1,)), ((), ())), preferred_element_type=F32
    )
    block[:, width:] = turned.astype(BF16)
    first[...] = block[: first.shape[0], :]


def norm(residual, projected, gain, expert_ids, route_weights, gathered):
    rows, width = residual.shape
    return call(
        norm_kernel,
        [
            jax.ShapeDtypeStruct((rows, width), F32),
            jax.ShapeDtypeStruct((rows, width + LANES), BF16),
            jax.ShapeDtypeStruct((min(rows, row_cuts(gathered)[1]), width + LANES), BF16),
        ],
        [residual, projected, gain.reshape(1, width), expert_ids.T, route_weights.T],
        [IN_VMEM] * 5,
        [],
        COVER,
        4 * MIB,
    )


def per_device(
    residual,
    queries,
    key_cache,
    value_cache,
    visible_len,
    out_weight,
    norm_gain,
    expert_ids,
    route_weights,
    w_gate,
    w_up,
    w_down,
):
    core, x, y, z, far = links()
    local_heads = queries.shape[1] // HD
    kv_index = lax.axis_index("head") * local_heads // (QH // KVH)
    kv, offsets = gather_keys(key_cache, value_cache, kv_index)
    projected = attention(queries, visible_len, kv, offsets, out_weight, residual.shape[0])
    dims = (x, y, z)
    hidden_state, block, first = norm(
        residual, projected, norm_gain, expert_ids, route_weights, residual.shape[0] << len(far)
    )
    matrices = (w_gate, w_up, w_down)
    own, got = spread(block, first, dims, far)
    own_c = [swap(p, core) for p in own]
    got_c = [swap(p, core) for p in got]
    top = expert_ids.shape[1]

    def run(parts, kind):
        return expert(parts, matrices, top, kind)

    def cut_up(value, parts):
        pieces, at = [], 0
        for p in parts:
            pieces.append(value[at : at + p.shape[0]])
            at += p.shape[0]
        return pieces

    back = swap(run(own_c, BF16), core)
    mine = cut_up(run(own, F32), own)
    kept = [m + b.astype(F32) for m, b in zip(mine, cut_up(back, own), strict=True)]
    sent = []
    for which in (slice(0, 1), slice(1, 3)):
        mine = run(got[which], F32)
        back = swap(run(got_c[which], BF16), core)
        sent += cut_up((mine + back.astype(F32)).astype(BF16), got[which])
    split = (sent, kept)
    mix = fold(*split, dims, far)
    return (hidden_state + mix).astype(BF16)


def solution(mesh):
    in_specs = (
        P(("qblk", "head"), None),
        P("qblk", "head"),
        P(None, "qblk", None),
        P(None, "qblk", None),
        P("qblk"),
        P("head", None),
        P(),
        P(("qblk", "head"), None),
        P(("qblk", "head"), None),
        P(("head", "qblk"), None, None),
        P(("head", "qblk"), None, None),
        P(("head", "qblk"), None, None),
    )
    out_specs = P(("qblk", "head"), None)

    return jax.shard_map(
        per_device, mesh=mesh, in_specs=in_specs, out_specs=out_specs, check_vma=False
    )
```
